32 devices in a mesh: bl: 8 (over y, x, core), ch: 4 (over z).
Axes of the slice: x: 2, y: 2, z: 4, core: 2. Of those that a mesh axis runs over, the one named last changes fastest.
Arguments:
- measured_correlations: float32 [2, 64, 16384], P(None, 'ch', 'bl'), may hold values from -6 to 6
- source_model_terms: float32 [2, 16, 64, 16384], P(None, None, 'ch', 'bl'), may hold values from -0.75 to 0.75
- stations: int32 [2, 16384], P(None, 'bl'), may hold values from 0 to 511, as said below
- initial_gains: float32 [2, 16, 64, 512], P(None, None, 'ch'), may hold values from -4 to 4
Outputs:
- gains: float32 [2, 16, 64, 512], P(None, None, 'ch')
- consensus: float32 [2, 16, 64, 512], P(None, None, 'ch')
The draws below stay inside these ranges and needn't reach their ends.
Inputs may be any that keep to these rules, and one draw needn't show every extreme that they name: Each baseline joins two different stations.
All inputs are finite; a program needn't handle non-finite values.
Results may differ from the reference program's by a relative error of at most 0.00025.
Values sent between devices are 32-bit elements; how exact they have to be, the bound alone decides.
A program may use at most 64 MiB of HBM per device.

```python
import jax
import jax.numpy as jnp
from jax import lax

RECEIVER_SITES = 512
SOURCE_PATCHES = 16
SPECTRAL_BINS = 64
PAIR_PORTION = 2048
ITERS = 3
PAIR_COUNT_ALL = 16384
N_BL = 8


def draw_stations(key, part):
    pair_start_receiver, pair_end_receiver = jax.random.split(key)
    start_receiver_number = jax.random.randint(pair_start_receiver, (PAIR_COUNT_ALL,), 0, RECEIVER_SITES)
    portion_starts = jax.random.randint(pair_end_receiver, (PAIR_COUNT_ALL,), 1, RECEIVER_SITES)
    right_ids = (start_receiver_number + portion_starts) % RECEIVER_SITES
    start_receiver_number = start_receiver_number.at[0].set(0)
    right_ids = right_ids.at[0].set(RECEIVER_SITES - 1)
    return jnp.stack([start_receiver_number, right_ids]).astype(jnp.int32)


def shard_levels(key, extent, cuts, smallest, top_value):
    def one(dim, shards_of):
        draws = jax.random.uniform(jax.random.fold_in(jax.random.fold_in(key, 6), dim), (shards_of,), jnp.float32, smallest / len(cuts), top_value / len(cuts))
        return jnp.repeat(jnp.exp(draws), extent[dim] // shards_of).reshape((-1,) + (1,) * (len(extent) - dim - 1))

    level = one(*cuts[0])
    for cut in cuts[1:]:
        level = level * one(*cut)
    return level


def gaussian(rng, extent, spread, bound, shards=(), kind=jnp.bfloat16):
    level = shard_levels(rng, extent, shards, -0.22, 0.18) if shards else 1.0
    array = jax.random.normal(rng, extent, jnp.float32) * spread * level
    return jnp.minimum(jnp.maximum(array, -bound), bound).astype(kind)


def setup_inputs(seed: int = 0) -> dict:
    arg_keys = jax.random.split(jax.random.key(seed), 5)
    return {
        "measured_correlations": gaussian(arg_keys[0], (2, SPECTRAL_BINS, PAIR_COUNT_ALL), 1.0, 6.0, ((1, 4), (2, 8)), jnp.float32),
        "source_model_terms": gaussian(arg_keys[1], (2, SOURCE_PATCHES, SPECTRAL_BINS, PAIR_COUNT_ALL), (2 * PAIR_PORTION * N_BL // RECEIVER_SITES) ** -0.5, 0.75, ((2, 4), (3, 8)), jnp.float32),
        "stations": draw_stations(jax.random.fold_in(arg_keys[4], 71), 0),
        "initial_gains": gaussian(arg_keys[3], (2, SOURCE_PATCHES, SPECTRAL_BINS, RECEIVER_SITES), 1.0, 4.0, ((2, 4),), jnp.float32),
    }


penalty = 1.0

def legendre_basis(channel_count):
    abscissa = -1.0 + 2.0 * jnp.arange(channel_count, dtype=jnp.float32) / (channel_count - 1)
    columns = []
    for degree in range(4):
        vector = abscissa ** degree
        for earlier in columns:
            vector = vector - jnp.sum(earlier * vector) * earlier
        vector = vector / jnp.sqrt(jnp.sum(vector * vector))
        columns.append(vector)
    return jnp.stack(columns, axis=1)

def complex_terms(measured_correlations, source_model_terms, gain_left, gain_right):
    m_real, m_imag = (source_model_terms[0], source_model_terms[1])
    left_re, left_im = (gain_left[0], gain_left[1])
    right_re, right_im = (gain_right[0], gain_right[1])
    a_real = m_real * right_re + m_imag * right_im
    a_imag = m_imag * right_re - m_real * right_im
    pred_re = left_re * a_real - left_im * a_imag
    pred_im = left_re * a_imag + left_im * a_real
    resid_re = measured_correlations[0] - lax.optimization_barrier(jnp.sum(pred_re, axis=0))
    resid_im = measured_correlations[1] - lax.optimization_barrier(jnp.sum(pred_im, axis=0))
    y_real = resid_re[None] + pred_re
    y_imag = resid_im[None] + pred_im
    left_terms = jnp.stack([y_real * a_real + y_imag * a_imag, y_imag * a_real - y_real * a_imag, a_real * a_real + a_imag * a_imag])
    b_real = m_real * left_re - m_imag * left_im
    b_imag = m_real * left_im + m_imag * left_re
    right_terms = jnp.stack([y_real * b_real + y_imag * b_imag, y_real * b_imag - y_imag * b_real, b_real * b_real + b_imag * b_imag])
    return (left_terms, right_terms)

def update_gains(totals, consensus, dual):
    factor = 1.0 / (totals[2] + penalty)
    return jnp.stack([(totals[0] + penalty * (consensus[0] - dual[0])) * factor, (totals[1] + penalty * (consensus[1] - dual[1])) * factor])

def station_scatter(terms, station_ids):
    moved = jnp.moveaxis(terms, 3, 0)
    summed = jax.ops.segment_sum(moved, station_ids, num_segments=RECEIVER_SITES)
    return jnp.moveaxis(summed, 0, 3)

def reference(measured_correlations, source_model_terms, stations, initial_gains):
    basis = legendre_basis(SPECTRAL_BINS)
    gains = initial_gains
    consensus = initial_gains
    dual = jnp.zeros_like(initial_gains)
    start_receiver_number = stations[0]
    right_ids = stations[1]
    for iteration in range(ITERS):
        gain_left = jnp.take(gains, start_receiver_number, axis=3)
        gain_right = jnp.take(gains, right_ids, axis=3)
        left_terms, right_terms = complex_terms(measured_correlations, source_model_terms, gain_left, gain_right)
        totals = station_scatter(left_terms, start_receiver_number) + station_scatter(right_terms, right_ids)
        gains = update_gains(totals, consensus, dual)
        shifted = gains + dual
        coeffs = jnp.einsum('fk,rdfs->rdks', basis, shifted, precision=lax.Precision.HIGHEST)
        consensus = jnp.einsum('fk,rdks->rdfs', basis, coeffs, precision=lax.Precision.HIGHEST)
        dual = shifted - consensus
    return (gains, consensus)
```

```python
import functools

import jax
import jax.numpy as jnp
import numpy as np
from jax import lax
from jax.experimental import pallas as pl
from jax.experimental.pallas import tpu as pltpu
from jax.sharding import PartitionSpec as P

SPECTRAL_BINS = 64
ITERS = 3
penalty = 1.0
MESH = pl.DeviceIdType.MESH
BLOCK = 512
CH = 8
LAG = 2


def legendre_basis(channel_count):
    steps = np.arange(channel_count, dtype=np.float32)
    abscissa = np.float32(-1.0) + np.float32(2.0) * steps / np.float32(channel_count - 1)
    columns = []
    for degree in range(4):
        vector = abscissa**degree
        for earlier in columns:
            vector = vector - np.sum(earlier * vector) * earlier
        vector = vector / np.sqrt(np.sum(vector * vector))
        columns.append(vector.astype(np.float32))
    return np.stack(columns, axis=1)


def split(value):
    high = value.astype(jnp.bfloat16)
    return high, (value - high.astype(jnp.float32)).astype(jnp.bfloat16)


def admm_kernel(
    cfg, vis_hbm, model_hbm, ids_hbm, init_hbm, basis_ref, out_g, out_c,
    vbuf, mbuf, ibuf, hot, hot_t, pieces, gbuf, res, tacc, acc, rsbuf, gains, cons, dual, shif,
    cpart, zbuf, zsum, sbuf, cfull,
    ld_sem, x_send, x_recv, rs_send, rs_recv, ag_send, ag_recv, z_send, z_recv, s_send, s_recv,
    k_send, k_recv, o_send, o_recv,
):
    ns, m, n_ch, n_dir, n_base = cfg
    n_st = init_hbm.shape[3]
    me = lax.axis_index("bl")
    ch = lax.axis_index("ch")
    core = lax.rem(me, ns)
    gi = me // ns
    sib = (me + 1 - 2 * core, ch)
    e = max(1, n_dir // (4 * m))
    me_d = m * e
    n_chunks = n_dir // me_d
    nbs = n_base // BLOCK
    n_blk = ns * nbs
    last = ITERS - 1

    def peer(t):
        return (lax.rem(gi + t, m) * ns + core, ch)

    def zpeer(t):
        return (me, lax.rem(ch + t, n_ch))

    others = [peer(t) for t in range(1, m)] + [zpeer(t) for t in range(1, n_ch)]
    if ns == 2:
        others.append(sib)
    barrier = pltpu.get_barrier_semaphore()
    for dev in others:
        pl.semaphore_signal(barrier, inc=1, device_id=dev, device_id_type=MESH)

    own = pl.ds(pl.multiple_of(core * CH, CH), CH)
    theirs = pl.ds(pl.multiple_of((ns - 1 - core) * CH, CH), CH)
    loads = [
        pltpu.make_async_copy(ids_hbm, ibuf.at[core], ld_sem.at[0]),
        pltpu.make_async_copy(init_hbm.at[0, :, own], gains.at[:, 0], ld_sem.at[1]),
        pltpu.make_async_copy(init_hbm.at[1, :, own], gains.at[:, 1], ld_sem.at[2]),
        pltpu.make_async_copy(vis_hbm.at[:, own], vbuf.at[core], ld_sem.at[3]),
        pltpu.make_async_copy(model_hbm.at[:, :, own], mbuf.at[core], ld_sem.at[4]),
    ]
    for copy in loads:
        copy.start()

    def remote(src, dst, send, recv, dev):
        return pltpu.make_async_remote_copy(
            src_ref=src, dst_ref=dst, send_sem=send, recv_sem=recv,
            device_id=dev, device_id_type=MESH,
        )

    pl.semaphore_wait(barrier, len(others))
    loads[0].wait()
    swaps = []
    if ns == 2:
        swaps = [
            remote(ibuf.at[core], ibuf.at[core], x_send.at[0], x_recv.at[0], sib),
            remote(vis_hbm.at[:, theirs], vbuf.at[core], x_send.at[1], x_recv.at[1], sib),
            remote(model_hbm.at[:, :, theirs], mbuf.at[core], x_send.at[2], x_recv.at[2], sib),
        ]
        for copy in swaps:
            copy.start()

    def build(src):
        def body(b, _):
            for side in range(2):
                row = ibuf[src, pl.ds(side, 1), pl.ds(pl.multiple_of(b * BLOCK, BLOCK), BLOCK)]
                station = lax.broadcasted_iota(jnp.int32, (n_st, BLOCK), 0)
                one = (station == row).astype(jnp.float32).astype(jnp.bfloat16)
                hot[src * nbs + b, :, pl.ds(side * BLOCK, BLOCK)] = one
                for i in range(BLOCK // 128):
                    col = jnp.transpose(
                        jnp.broadcast_to(row[:, i * 128 : (i + 1) * 128], (128, 128))
                    )
                    lane = lax.broadcasted_iota(jnp.int32, (128, 128), 1)
                    for j in range(n_st // 128):
                        one = (col == lane + j * 128).astype(jnp.float32).astype(jnp.bfloat16)
                        where = pl.ds(side * BLOCK + i * 128, 128)
                        hot_t[src * nbs + b, where, pl.ds(j * 128, 128)] = one
            return 0

        lax.fori_loop(0, nbs, body, 0)

    build(core)
    if ns == 2:
        swaps[0].wait_recv()
        build(1 - core)
    for copy in loads[1:]:
        copy.wait()
    for copy in swaps[1:]:
        copy.wait_recv()

    for k in range(n_chunks):
        for i in range(e):
            cons[k * e + i] = gains[k * me_d + gi * e + i]
    dual[...] = jnp.zeros_like(dual)

    def own_dirs(k):
        return pl.ds(k * me_d + gi * e, e)

    def rs_copy(k, t):
        return remote(
            acc.at[k, pl.ds(lax.rem(gi + t, m) * e, e)], rsbuf.at[k, t - 1],
            rs_send.at[k, t - 1], rs_recv.at[k, t - 1], peer(t),
        )

    def ag_copy(k, t):
        return remote(
            gains.at[own_dirs(k)], gains.at[own_dirs(k)],
            ag_send.at[k, t - 1], ag_recv.at[k, t - 1], peer(t),
        )

    def z_copy(par, k, t):
        return remote(
            cpart.at[par, k], zbuf.at[par, k, t - 1],
            z_send.at[par, k, t - 1], z_recv.at[par, k, t - 1], zpeer(t),
        )

    def s_copy(par, k):
        return remote(
            zsum.at[par, k], sbuf.at[par, k], s_send.at[par, k], s_recv.at[par, k], sib
        )

    def k_copy(k, t):
        return remote(
            cfull.at[own_dirs(k)], cfull.at[own_dirs(k)],
            k_send.at[k, t - 1], k_recv.at[k, t - 1], peer(t),
        )

    def gather_chunk(k):
        for i in range(me_d):
            d = k * me_d + i
            high, low = split(gains[d].reshape(2 * CH, n_st))
            pieces[pl.ds(i * 2 * CH, 2 * CH), :] = high
            pieces[pl.ds((me_d + i) * 2 * CH, 2 * CH), :] = low

        def body(b, _):
            src = b // nbs
            lanes = pl.ds(pl.multiple_of(lax.rem(b, nbs) * BLOCK, BLOCK), BLOCK)
            both = jnp.dot(pieces[...], hot[b], preferred_element_type=jnp.float32)
            half = me_d * 2 * CH
            res_re = res[b, 0]
            res_im = res[b, 1]
            for i in range(me_d):
                d = k * me_d + i
                lo = i * 2 * CH
                g = both[lo : lo + 2 * CH] + both[half + lo : half + lo + 2 * CH]
                gbuf[d, b] = g
                l_re, l_im = g[:CH, :BLOCK], g[CH:, :BLOCK]
                r_re, r_im = g[:CH, BLOCK:], g[CH:, BLOCK:]
                m_re, m_im = mbuf[src, 0, d, :, lanes], mbuf[src, 1, d, :, lanes]
                a_re = m_re * r_re + m_im * r_im
                a_im = m_im * r_re - m_re * r_im
                res_re = res_re - (l_re * a_re - l_im * a_im)
                res_im = res_im - (l_re * a_im + l_im * a_re)
            res[b, 0] = res_re
            res[b, 1] = res_im
            return 0

        lax.fori_loop(0, n_blk, body, 0)

    def scatter_chunk(k):
        tacc[...] = jnp.zeros_like(tacc)

        def body(b, _):
            src = b // nbs
            lanes = pl.ds(pl.multiple_of(lax.rem(b, nbs) * BLOCK, BLOCK), BLOCK)
            res_re = res[b, 0]
            res_im = res[b, 1]
            highs, lows, w_high, w_low = [], [], [], []
            sides = [[], []]
            for i in range(me_d):
                d = k * me_d + i
                m_re, m_im = mbuf[src, 0, d, :, lanes], mbuf[src, 1, d, :, lanes]
                t_re = res_re * m_re + res_im * m_im
                t_im = res_re * m_im - res_im * m_re
                power = m_re * m_re + m_im * m_im
                for side in range(2):
                    other = pl.ds((1 - side) * BLOCK, BLOCK)
                    g_re = gbuf[d, b, pl.ds(0, CH), other]
                    g_im = gbuf[d, b, pl.ds(CH, CH), other]
                    if side == 0:
                        re = t_re * g_re + t_im * g_im
                        im = t_re * g_im - t_im * g_re
                    else:
                        re = t_re * g_re - t_im * g_im
                        im = t_re * g_im + t_im * g_re
                    w = power * (g_re * g_re + g_im * g_im)
                    sides[side].append((re, im, w))
            parts = []
            for side in range(2):
                num_h, num_l = [], []
                for re, im, _w in sides[side]:
                    high, low = split(jnp.concatenate([re, im], axis=0))
                    num_h.append(high)
                    num_l.append(low)
                for i in range(0, me_d, 2):
                    pair = [sides[side][i][2], sides[side][i + 1][2]]
                    high, low = split(jnp.concatenate(pair, axis=0))
                    num_h.append(high)
                    num_l.append(low)
                parts.append(jnp.concatenate(num_h + num_l, axis=0))
            terms = jnp.concatenate(parts, axis=1)
            tacc[...] += jnp.dot(terms, hot_t[b], preferred_element_type=jnp.float32)
            return 0

        lax.fori_loop(0, n_blk, body, 0)
        half = me_d * 3 * CH
        for i in range(me_d):
            a, w = i * 2 * CH, me_d * 2 * CH + i * CH
            acc[k, i, pl.ds(0, 2 * CH), :] = (
                tacc[pl.ds(a, 2 * CH), :] + tacc[pl.ds(half + a, 2 * CH), :]
            )
            acc[k, i, pl.ds(2 * CH, CH), :] = (
                tacc[pl.ds(w, CH), :] + tacc[pl.ds(half + w, CH), :]
            )
        for t in range(1, m):
            rs_copy(k, t).start()

    def wide(table, degree):
        return jnp.concatenate([basis_ref[table, degree]] * (n_st // 128), axis=1)

    table = ch * ns + core

    def update(it, par, k):
        for t in range(1, m):
            rs_copy(k, t).wait_recv()

        @pl.when(it > 0)
        def _():
            for t in range(1, m):
                ag_copy(k, t).wait_send()

        for i in range(e):
            o = k * e + i
            d = k * me_d + gi * e + i
            total = acc[k, gi * e + i]
            for t in range(1, m):
                total = total + rsbuf[k, t - 1, i]
            weight = total[2 * CH :]
            factor = 1.0 / (weight + penalty)
            rows = [None] * 8
            for part in range(2):
                num = total[part * CH : (part + 1) * CH] + gains[d, part] * weight
                new = (num + penalty * (cons[o, part] - dual[o, part])) * factor
                gains[d, part] = new
                shifted = new + dual[o, part]
                shif[o, part] = shifted
                for degree in range(4):
                    rows[degree * 2 + part] = jnp.sum(
                        shifted * wide(table, degree), axis=0, keepdims=True
                    )
            cpart[par, k, i] = jnp.concatenate(rows, axis=0)
        for t in range(1, m):
            ag_copy(k, t).start()
        for t in range(1, n_ch):
            z_copy(par, k, t).start()
        for t in range(1, m):
            rs_copy(k, t).wait_send()

    def fit_sum(par, k):
        for t in range(1, n_ch):
            z_copy(par, k, t).wait_recv()
        value = cpart[par, k]
        for t in range(1, n_ch):
            value = value + zbuf[par, k, t - 1]
        zsum[par, k] = value
        if ns == 2:
            s_copy(par, k).start()
        for t in range(1, n_ch):
            z_copy(par, k, t).wait_send()

    def fit_total(par, k):
        value = zsum[par, k]
        if ns == 2:
            s_copy(par, k).wait_recv()
            value = value + sbuf[par, k]
            s_copy(par, k).wait_send()
        return value

    def fit(par, k):
        value = fit_total(par, k)
        for i in range(e):
            o = k * e + i
            for part in range(2):
                line = wide(table, 0) * value[i, part : part + 1]
                for degree in range(1, 4):
                    at = degree * 2 + part
                    line = line + wide(table, degree) * value[i, at : at + 1]
                cons[o, part] = line
                dual[o, part] = shif[o, part] - line

    def iteration(it, _):
        par = lax.rem(it, 2)
        before = 1 - par
        for b in range(n_blk):
            src, lanes = b // nbs, pl.ds((b % nbs) * BLOCK, BLOCK)
            res[b] = vbuf[src, :, :, lanes]

        def gather_step(k, _):
            @pl.when(it > 0)
            def _():
                for t in range(1, m):
                    ag_copy(k, t).wait_recv()

            gather_chunk(k)

            @pl.when(it > 0)
            def _():
                fit_sum(before, k)

            return 0

        lax.fori_loop(0, n_chunks, gather_step, 0)

        def scatter_step(k, _):
            @pl.when(it > 0)
            def _():
                fit(before, k)

            scatter_chunk(k)

            @pl.when(k >= LAG)
            def _():
                update(it, par, k - LAG)

            return 0

        lax.fori_loop(0, n_chunks, scatter_step, 0)
        for k in range(max(0, n_chunks - LAG), n_chunks):
            update(it, par, k)
        return 0

    lax.fori_loop(0, ITERS, iteration, 0)

    par = last % 2
    for k in range(n_chunks):
        fit_sum(par, k)
    for k in range(n_chunks):
        value = fit_total(par, k)
        cfull[own_dirs(k)] = value
        for t in range(1, m):
            k_copy(k, t).start()

    def o_copy(k, part):
        dirs = pl.ds(k * me_d, me_d)
        return remote(
            gains.at[dirs, part], out_g.at[part, dirs, own],
            o_send.at[k, part], o_recv.at[k, part], sib,
        )

    for k in range(n_chunks):
        for t in range(1, m):
            ag_copy(k, t).wait_recv()
        for part in range(2):
            if ns == 2:
                o_copy(k, part).start()
            for i in range(me_d):
                out_g[part, k * me_d + i, own, :] = gains[k * me_d + i, part]
    for k in range(n_chunks):
        for t in range(1, m):
            k_copy(k, t).wait_recv()
        for i in range(me_d):
            d = k * me_d + i
            for h in range(ns):
                for part in range(2):
                    line = wide(ch * ns + h, 0) * cfull[d, pl.ds(part, 1)]
                    for degree in range(1, 4):
                        line = line + wide(ch * ns + h, degree) * cfull[d, pl.ds(degree * 2 + part, 1)]
                    out_c[part, d, pl.ds(h * CH, CH), :] = line
    for k in range(n_chunks):
        for t in range(1, m):
            ag_copy(k, t).wait_send()
            k_copy(k, t).wait_send()
        if ns == 2:
            for part in range(2):
                o_copy(k, part).wait_recv()
                o_copy(k, part).wait_send()
    for copy in swaps:
        copy.wait_send()


def per_device(n, n_ch, vis, model, stations, initial_gains):
    n_dir, n_chan, n_st = initial_gains.shape[1:]
    n_base = model.shape[3]
    ns = n_chan // CH
    m = n // ns
    e = max(1, n_dir // (4 * m))
    me_d = m * e
    n_chunks = n_dir // me_d
    n_own = n_chunks * e
    n_blk = ns * n_base // BLOCK
    table = legendre_basis(SPECTRAL_BINS).reshape(SPECTRAL_BINS // CH, CH, 4).transpose(0, 2, 1)
    basis = jnp.asarray(np.ascontiguousarray(np.broadcast_to(table[..., None], table.shape + (128,))))
    f32, bf16 = jnp.float32, jnp.bfloat16
    dma = pltpu.SemaphoreType.DMA
    vmem = pl.BlockSpec(memory_space=pltpu.VMEM)
    hbm = pl.BlockSpec(memory_space=pl.ANY)
    out = jax.ShapeDtypeStruct(initial_gains.shape, f32)
    return pl.pallas_call(
        functools.partial(admm_kernel, (ns, m, n_ch, n_dir, n_base)),
        out_shape=(out, out),
        in_specs=[hbm, hbm, hbm, hbm, vmem],
        out_specs=(vmem, vmem),
        scratch_shapes=[
            pltpu.VMEM((ns, 2, CH, n_base), f32),
            pltpu.VMEM((ns, 2, n_dir, CH, n_base), f32),
            pltpu.VMEM((ns, 2, n_base), jnp.int32),
            pltpu.VMEM((n_blk, n_st, 2 * BLOCK), bf16),
            pltpu.VMEM((n_blk, 2 * BLOCK, n_st), bf16),
            pltpu.VMEM((4 * me_d * CH, n_st), bf16),
            pltpu.VMEM((n_dir, n_blk, 2 * CH, 2 * BLOCK), f32),
            pltpu.VMEM((n_blk, 2, CH, BLOCK), f32),
            pltpu.VMEM((6 * me_d * CH, n_st), f32),
            pltpu.VMEM((n_chunks, me_d, 3 * CH, n_st), f32),
            pltpu.VMEM((n_chunks, m - 1, e, 3 * CH, n_st), f32),
            pltpu.VMEM((n_dir, 2, CH, n_st), f32),
            pltpu.VMEM((n_own, 2, CH, n_st), f32),
            pltpu.VMEM((n_own, 2, CH, n_st), f32),
            pltpu.VMEM((n_own, 2, CH, n_st), f32),
            pltpu.VMEM((2, n_chunks, e, 8, n_st), f32),
            pltpu.VMEM((2, n_chunks, n_ch - 1, e, 8, n_st), f32),
            pltpu.VMEM((2, n_chunks, e, 8, n_st), f32),
            pltpu.VMEM((2, n_chunks, e, 8, n_st), f32),
            pltpu.VMEM((n_dir, 8, n_st), f32),
            dma((5,)),
            dma((3,)),
            dma((3,)),
            dma((n_chunks, m - 1)),
            dma((n_chunks, m - 1)),
            dma((n_chunks, m - 1)),
            dma((n_chunks, m - 1)),
            dma((2, n_chunks, n_ch - 1)),
            dma((2, n_chunks, n_ch - 1)),
            dma((2, n_chunks)),
            dma((2, n_chunks)),
            dma((n_chunks, m - 1)),
            dma((n_chunks, m - 1)),
            dma((n_chunks, 2)),
            dma((n_chunks, 2)),
        ],
        compiler_params=pltpu.CompilerParams(
            collective_id=0, has_side_effects=True, vmem_limit_bytes=56 * 2**20
        ),
        name="admm",
    )(vis, model, stations, initial_gains, basis)


def solution(mesh):
    placed = (
        P(None, "ch", "bl"),
        P(None, None, "ch", "bl"),
        P(None, "bl"),
        P(None, None, "ch", None),
    )
    return jax.shard_map(
        functools.partial(per_device, mesh.shape["bl"], mesh.shape["ch"]),
        mesh=mesh,
        in_specs=placed,
        out_specs=(P(None, None, "ch", None), P(None, None, "ch", None)),
        check_vma=False,
    )
```

```python
import functools

import jax
import jax.numpy as jnp
import numpy as np
from jax import lax
from jax.experimental import pallas as pl
from jax.experimental.pallas import tpu as pltpu
from jax.sharding import PartitionSpec as P

SPECTRAL_BINS = 64
ITERS = 3
penalty = 1.0
MESH = pl.DeviceIdType.MESH
BLOCK = 512
CH = 8
FINISH_STEPS = 2


def legendre_basis(channel_count):
    steps = np.arange(channel_count, dtype=np.float32)
    abscissa = np.float32(-1.0) + np.float32(2.0) * steps / np.float32(channel_count - 1)
    columns = []
    for degree in range(4):
        vector = abscissa**degree
        for earlier in columns:
            vector = vector - np.sum(earlier * vector) * earlier
        vector = vector / np.sqrt(np.sum(vector * vector))
        columns.append(vector.astype(np.float32))
    return np.stack(columns, axis=1)


def split(value):
    high = value.astype(jnp.bfloat16)
    return high, (value - high.astype(jnp.float32)).astype(jnp.bfloat16)


def admm_kernel(
    cfg, vis_hbm, model_hbm, ids_hbm, init_hbm, basis_ref, out_g, cfull,
    vbuf, mbuf, ibuf, hot, hot_t, pieces, gbuf, res, tacc, acc, rsbuf, gains, cons, dual, shif,
    cpart, zbuf, zsum, sbuf, ctot,
    ld_sem, m_load, x_send, x_recv, m_send, m_recv, rs_send, rs_recv, ag_send, ag_recv, z_send, z_recv, s_send, s_recv,
    k_send, k_recv, o_send, o_recv, g_sem, c_sem,
):
    ns, m, n_ch, n_dir, n_base = cfg
    n_st = init_hbm.shape[3]
    me = lax.axis_index("bl")
    ch = lax.axis_index("ch")
    core = lax.rem(me, ns)
    gi = me // ns
    sib = (me + 1 - 2 * core, ch)
    e = max(1, n_dir // (4 * m))
    me_d = m * e
    n_chunks = n_dir // me_d
    nbs = n_base // BLOCK
    n_blk = ns * nbs
    last = ITERS - 1
    lag = max(1, n_chunks - 1)
    held = n_chunks - 1 if n_chunks > 1 else n_chunks

    def peer(t):
        return (lax.rem(gi + t, m) * ns + core, ch)

    def zpeer(t):
        return (me, lax.rem(ch + t, n_ch))

    others = [peer(t) for t in range(1, m)] + [zpeer(t) for t in range(1, n_ch)]
    if ns == 2:
        others.append(sib)
    barrier = pltpu.get_barrier_semaphore()
    for dev in others:
        pl.semaphore_signal(barrier, inc=1, device_id=dev, device_id_type=MESH)

    own = pl.ds(pl.multiple_of(core * CH, CH), CH)
    theirs = pl.ds(pl.multiple_of((ns - 1 - core) * CH, CH), CH)
    loads = [
        pltpu.make_async_copy(ids_hbm, ibuf.at[core], ld_sem.at[0]),
        pltpu.make_async_copy(init_hbm.at[0, :, own], gains.at[:, 0], ld_sem.at[1]),
        pltpu.make_async_copy(init_hbm.at[1, :, own], gains.at[:, 1], ld_sem.at[2]),
        pltpu.make_async_copy(vis_hbm.at[:, own], vbuf.at[core], ld_sem.at[3]),
    ]
    for copy in loads:
        copy.start()

    def model_load(k):
        dirs = pl.ds(k * me_d, me_d)
        return pltpu.make_async_copy(
            model_hbm.at[:, dirs, own], mbuf.at[core, :, dirs], m_load.at[k]
        )

    for k in range(n_chunks):
        model_load(k).start()

    def remote(src, dst, send, recv, dev):
        return pltpu.make_async_remote_copy(
            src_ref=src, dst_ref=dst, send_sem=send, recv_sem=recv,
            device_id=dev, device_id_type=MESH,
        )

    def build(src):
        def body(b, _):
            for side in range(2):
                row = ibuf[src, pl.ds(side, 1), pl.ds(pl.multiple_of(b * BLOCK, BLOCK), BLOCK)]
                station = lax.broadcasted_iota(jnp.int32, (n_st, BLOCK), 0)
                one = (station == row).astype(jnp.float32).astype(jnp.bfloat16)
                hot[src * nbs + b, :, pl.ds(side * BLOCK, BLOCK)] = one
            return 0

        lax.fori_loop(0, nbs, body, 0, unroll=nbs)

    def build_t(src):
        def body(b, _):
            for side in range(2):
                row = ibuf[src, pl.ds(side, 1), pl.ds(pl.multiple_of(b * BLOCK, BLOCK), BLOCK)]
                for i in range(BLOCK // 128):
                    col = jnp.transpose(
                        jnp.broadcast_to(row[:, i * 128 : (i + 1) * 128], (128, 128))
                    )
                    lane = lax.broadcasted_iota(jnp.int32, (128, 128), 1)
                    for j in range(n_st // 128):
                        one = (col == lane + j * 128).astype(jnp.float32).astype(jnp.bfloat16)
                        where = pl.ds(side * BLOCK + i * 128, 128)
                        hot_t[src * nbs + b, where, pl.ds(j * 128, 128)] = one
            return 0

        lax.fori_loop(0, nbs, body, 0, unroll=nbs)

    loads[0].wait()
    build(core)
    pl.semaphore_wait(barrier, len(others))
    swaps = []
    if ns == 2:
        swaps = [
            remote(ibuf.at[core], ibuf.at[core], x_send.at[0], x_recv.at[0], sib),
            remote(vis_hbm.at[:, theirs], vbuf.at[core], x_send.at[1], x_recv.at[1], sib),
        ]

    def model_swap(k):
        dirs = pl.ds(k * me_d, me_d)
        return remote(
            model_hbm.at[:, dirs, theirs], mbuf.at[core, :, dirs], m_send.at[k], m_recv.at[k], sib
        )

    if ns == 2:
        for copy in swaps:
            copy.start()
        for k in range(n_chunks):
            model_swap(k).start()

    build_t(core)
    if ns == 2:
        swaps[0].wait_recv()
        build(1 - core)
        build_t(1 - core)
    for copy in loads[1:]:
        copy.wait()
    for copy in swaps[1:]:
        copy.wait_recv()

    for k in range(n_chunks):
        for i in range(e):
            cons[k * e + i] = gains[k * me_d + gi * e + i]
    dual[...] = jnp.zeros_like(dual)

    def own_dirs(k):
        return pl.ds(k * me_d + gi * e, e)

    def rs_copy(k, t):
        return remote(
            acc.at[k, pl.ds(lax.rem(gi + t, m) * e, e)], rsbuf.at[k, t - 1],
            rs_send.at[k, t - 1], rs_recv.at[k, t - 1], peer(t),
        )

    def ag_copy(k, t):
        return remote(
            gains.at[own_dirs(k)], gains.at[own_dirs(k)],
            ag_send.at[k, t - 1], ag_recv.at[k, t - 1], peer(t),
        )

    def z_copy(par, k, t):
        return remote(
            cpart.at[par, k], zbuf.at[par, k, t - 1],
            z_send.at[par, k, t - 1], z_recv.at[par, k, t - 1], zpeer(t),
        )

    def s_copy(par, k):
        return remote(
            zsum.at[par, k], sbuf.at[par, k], s_send.at[par, k], s_recv.at[par, k], sib
        )

    def k_copy(k, t):
        return remote(
            ctot.at[k], cfull.at[own_dirs(k)],
            k_send.at[k, t - 1], k_recv.at[k, t - 1], peer(t),
        )

    def gather_chunk(k):
        for i in range(me_d):
            d = k * me_d + i
            high, low = split(gains[d].reshape(2 * CH, n_st))
            pieces[pl.ds(i * 2 * CH, 2 * CH), :] = high
            pieces[pl.ds((me_d + i) * 2 * CH, 2 * CH), :] = low

        def body(b, _):
            src = b // nbs
            lanes = pl.ds(pl.multiple_of(lax.rem(b, nbs) * BLOCK, BLOCK), BLOCK)
            both = jnp.dot(pieces[...], hot[b], preferred_element_type=jnp.float32)
            half = me_d * 2 * CH
            res_re = res[b, 0]
            res_im = res[b, 1]
            for i in range(me_d):
                d = k * me_d + i
                lo = i * 2 * CH
                g = both[lo : lo + 2 * CH] + both[half + lo : half + lo + 2 * CH]
                gbuf[d, b] = g
                l_re, l_im = g[:CH, :BLOCK], g[CH:, :BLOCK]
                r_re, r_im = g[:CH, BLOCK:], g[CH:, BLOCK:]
                m_re, m_im = mbuf[src, 0, d, :, lanes], mbuf[src, 1, d, :, lanes]
                a_re = m_re * r_re + m_im * r_im
                a_im = m_im * r_re - m_re * r_im
                res_re = res_re - (l_re * a_re - l_im * a_im)
                res_im = res_im - (l_re * a_im + l_im * a_re)
            res[b, 0] = res_re
            res[b, 1] = res_im
            return 0

        lax.fori_loop(0, n_blk, body, 0, unroll=n_blk)

    def scatter_chunk(k):
        tacc[...] = jnp.zeros_like(tacc)

        def body(b, _):
            src = b // nbs
            lanes = pl.ds(pl.multiple_of(lax.rem(b, nbs) * BLOCK, BLOCK), BLOCK)
            res_re = res[b, 0]
            res_im = res[b, 1]
            highs, lows, w_high, w_low = [], [], [], []
            sides = [[], []]
            for i in range(me_d):
                d = k * me_d + i
                m_re, m_im = mbuf[src, 0, d, :, lanes], mbuf[src, 1, d, :, lanes]
                t_re = res_re * m_re + res_im * m_im
                t_im = res_re * m_im - res_im * m_re
                power = m_re * m_re + m_im * m_im
                for side in range(2):
                    other = pl.ds((1 - side) * BLOCK, BLOCK)
                    g_re = gbuf[d, b, pl.ds(0, CH), other]
                    g_im = gbuf[d, b, pl.ds(CH, CH), other]
                    if side == 0:
                        re = t_re * g_re + t_im * g_im
                        im = t_re * g_im - t_im * g_re
                    else:
                        re = t_re * g_re - t_im * g_im
                        im = t_re * g_im + t_im * g_re
                    w = power * (g_re * g_re + g_im * g_im)
                    sides[side].append((re, im, w))
            parts = []
            for side in range(2):
                num_h, num_l = [], []
                for re, im, _w in sides[side]:
                    high, low = split(jnp.concatenate([re, im], axis=0))
                    num_h.append(high)
                    num_l.append(low)
                for i in range(0, me_d, 2):
                    pair = [sides[side][i][2], sides[side][i + 1][2]]
                    high, low = split(jnp.concatenate(pair, axis=0))
                    num_h.append(high)
                    num_l.append(low)
                parts.append(jnp.concatenate(num_h + num_l, axis=0))
            terms = jnp.concatenate(parts, axis=1)
            tacc[...] += jnp.dot(terms, hot_t[b], preferred_element_type=jnp.float32)
            return 0

        lax.fori_loop(0, n_blk, body, 0, unroll=n_blk)
        half = me_d * 3 * CH
        for i in range(me_d):
            a, w = i * 2 * CH, me_d * 2 * CH + i * CH
            acc[k, i, pl.ds(0, 2 * CH), :] = (
                tacc[pl.ds(a, 2 * CH), :] + tacc[pl.ds(half + a, 2 * CH), :]
            )
            acc[k, i, pl.ds(2 * CH, CH), :] = (
                tacc[pl.ds(w, CH), :] + tacc[pl.ds(half + w, CH), :]
            )
        for t in range(1, m):
            rs_copy(k, t).start()

    def wide(table, degree):
        return jnp.concatenate([basis_ref[table, degree]] * (n_st // 128), axis=1)

    table = ch * ns + core

    def update(it, par, k):
        for t in range(1, m):
            rs_copy(k, t).wait_recv()

        @pl.when(it > 0)
        def _():
            for t in range(1, m):
                ag_copy(k, t).wait_send()

        @pl.when(it > 0)
        def _():
            fit(1 - par, k)

        for i in range(e):
            o = k * e + i
            d = k * me_d + gi * e + i
            total = acc[k, gi * e + i]
            for t in range(1, m):
                total = total + rsbuf[k, t - 1, i]
            weight = total[2 * CH :]
            factor = 1.0 / (weight + penalty)
            rows = [None] * 8
            for part in range(2):
                num = total[part * CH : (part + 1) * CH] + gains[d, part] * weight
                new = (num + penalty * (cons[o, part] - dual[o, part])) * factor
                gains[d, part] = new
                shifted = new + dual[o, part]
                shif[o, part] = shifted
                for degree in range(4):
                    rows[degree * 2 + part] = jnp.sum(
                        shifted * wide(table, degree), axis=0, keepdims=True
                    )
            cpart[par, k, i] = jnp.concatenate(rows, axis=0)
        for t in range(1, m):
            ag_copy(k, t).start()
        for t in range(1, n_ch):
            z_copy(par, k, t).start()
        for t in range(1, m):
            rs_copy(k, t).wait_send()

    def fit_sum(par, k):
        for t in range(1, n_ch):
            z_copy(par, k, t).wait_recv()
        value = cpart[par, k]
        for t in range(1, n_ch):
            value = value + zbuf[par, k, t - 1]
        zsum[par, k] = value
        if ns == 2:
            s_copy(par, k).start()
        for t in range(1, n_ch):
            z_copy(par, k, t).wait_send()

    def fit_total(par, k):
        value = zsum[par, k]
        if ns == 2:
            s_copy(par, k).wait_recv()
            value = value + sbuf[par, k]
            s_copy(par, k).wait_send()
        return value

    def fit(par, k):
        value = fit_total(par, k)
        for i in range(e):
            o = k * e + i
            for part in range(2):
                line = wide(table, 0) * value[i, part : part + 1]
                for degree in range(1, 4):
                    at = degree * 2 + part
                    line = line + wide(table, degree) * value[i, at : at + 1]
                cons[o, part] = line
                dual[o, part] = shif[o, part] - line

    def iteration(it, _):
        par = lax.rem(it, 2)
        before = 1 - par
        for b in range(n_blk):
            src, lanes = b // nbs, pl.ds((b % nbs) * BLOCK, BLOCK)
            res[b] = vbuf[src, :, :, lanes]

        def gather_step(k, _):
            if held < n_chunks:

                @pl.when((it > 0) & (k == 0))
                def _():
                    update(it - 1, before, held)

            @pl.when(it > 0)
            def _():
                for t in range(1, m):
                    ag_copy(k, t).wait_recv()

            @pl.when(it == 0)
            def _():
                model_load(k).wait()
                if ns == 2:
                    model_swap(k).wait_recv()

            gather_chunk(k)

            return 0

        lax.fori_loop(0, n_chunks, gather_step, 0)

        def scatter_step(k, _):
            scatter_chunk(k)

            @pl.when(it > 0)
            def _():
                fit_sum(before, k)

            @pl.when(k >= lag)
            def _():
                update(it, par, k - lag)

            return 0

        lax.fori_loop(0, n_chunks, scatter_step, 0)
        for k in range(max(0, n_chunks - lag), held):
            update(it, par, k)
        return 0

    lax.fori_loop(0, ITERS, iteration, 0)

    par = last % 2
    for k in range(held, n_chunks):
        update(last, par, k)

    def o_copy(k, part):
        dirs = pl.ds(k * me_d, me_d)
        return remote(
            gains.at[dirs, part], out_g.at[part, dirs, own],
            o_send.at[k, part], o_recv.at[k, part], sib,
        )

    def send_fit(k):
        ctot[k] = fit_total(par, k)
        pltpu.make_async_copy(ctot.at[k], cfull.at[own_dirs(k)], c_sem.at[k]).start()
        for t in range(1, m):
            k_copy(k, t).start()

    def g_copy(k, part):
        dirs = pl.ds(k * me_d, me_d)
        return pltpu.make_async_copy(
            gains.at[dirs, part], out_g.at[part, dirs, own], g_sem.at[k, part]
        )

    def give_gains(k):
        for t in range(1, m):
            ag_copy(k, t).wait_recv()
        for part in range(2):
            if ns == 2:
                o_copy(k, part).start()
            g_copy(k, part).start()

    for k in range(held):
        fit_sum(par, k)
    for k in range(held):
        send_fit(k)
        give_gains(k)
    for k in range(held, n_chunks):
        fit_sum(par, k)
        send_fit(k)
        give_gains(k)
    for k in range(n_chunks):
        for t in range(1, m):
            k_copy(k, t).wait_recv()
            ag_copy(k, t).wait_send()
            k_copy(k, t).wait_send()
        for part in range(2):
            g_copy(k, part).wait()
        pltpu.make_async_copy(ctot.at[k], cfull.at[own_dirs(k)], c_sem.at[k]).wait()
        if ns == 2:
            model_swap(k).wait_send()
            for part in range(2):
                o_copy(k, part).wait_recv()
                o_copy(k, part).wait_send()
    for copy in swaps:
        copy.wait_send()


def finish_kernel(ns, gains_ref, coef_ref, basis_ref, out_g, out_c):
    out_g[...] = gains_ref[...]
    n_dir, _, n_st = coef_ref.shape
    ch = lax.axis_index("ch")
    for h in range(ns):
        base = [
            jnp.concatenate([basis_ref[ch * ns + h, k]] * (n_st // 128), axis=1) for k in range(4)
        ]
        for d in range(n_dir):
            for part in range(2):
                line = base[0] * coef_ref[d, pl.ds(part, 1)]
                for k in range(1, 4):
                    line = line + base[k] * coef_ref[d, pl.ds(2 * k + part, 1)]
                out_c[part, d, pl.ds(h * CH, CH), :] = line


def per_device(n, n_ch, vis, model, stations, initial_gains):
    n_dir, n_chan, n_st = initial_gains.shape[1:]
    n_base = model.shape[3]
    ns = n_chan // CH
    m = n // ns
    e = max(1, n_dir // (4 * m))
    me_d = m * e
    n_chunks = n_dir // me_d
    n_own = n_chunks * e
    n_blk = ns * n_base // BLOCK
    table = legendre_basis(SPECTRAL_BINS).reshape(SPECTRAL_BINS // CH, CH, 4).transpose(0, 2, 1)
    basis = jnp.asarray(np.ascontiguousarray(np.broadcast_to(table[..., None], table.shape + (128,))))
    f32, bf16 = jnp.float32, jnp.bfloat16
    dma = pltpu.SemaphoreType.DMA
    vmem = pl.BlockSpec(memory_space=pltpu.VMEM)
    hbm = pl.BlockSpec(memory_space=pltpu.HBM)
    out = jax.ShapeDtypeStruct(initial_gains.shape, f32)
    fits = jax.ShapeDtypeStruct((n_dir, 8, n_st), f32)
    gains, coefs = pl.pallas_call(
        functools.partial(admm_kernel, (ns, m, n_ch, n_dir, n_base)),
        out_shape=(out, fits),
        in_specs=[hbm, hbm, hbm, hbm, vmem],
        out_specs=(hbm, hbm),
        scratch_shapes=[
            pltpu.VMEM((ns, 2, CH, n_base), f32),
            pltpu.VMEM((ns, 2, n_dir, CH, n_base), f32),
            pltpu.VMEM((ns, 2, n_base), jnp.int32),
            pltpu.VMEM((n_blk, n_st, 2 * BLOCK), bf16),
            pltpu.VMEM((n_blk, 2 * BLOCK, n_st), bf16),
            pltpu.VMEM((4 * me_d * CH, n_st), bf16),
            pltpu.VMEM((n_dir, n_blk, 2 * CH, 2 * BLOCK), f32),
            pltpu.VMEM((n_blk, 2, CH, BLOCK), f32),
            pltpu.VMEM((6 * me_d * CH, n_st), f32),
            pltpu.VMEM((n_chunks, me_d, 3 * CH, n_st), f32),
            pltpu.VMEM((n_chunks, m - 1, e, 3 * CH, n_st), f32),
            pltpu.VMEM((n_dir, 2, CH, n_st), f32),
            pltpu.VMEM((n_own, 2, CH, n_st), f32),
            pltpu.VMEM((n_own, 2, CH, n_st), f32),
            pltpu.VMEM((n_own, 2, CH, n_st), f32),
            pltpu.VMEM((2, n_chunks, e, 8, n_st), f32),
            pltpu.VMEM((2, n_chunks, n_ch - 1, e, 8, n_st), f32),
            pltpu.VMEM((2, n_chunks, e, 8, n_st), f32),
            pltpu.VMEM((2, n_chunks, e, 8, n_st), f32),
            pltpu.VMEM((n_chunks, e, 8, n_st), f32),
            dma((4,)),
            dma((n_chunks,)),
            dma((2,)),
            dma((2,)),
            dma((n_chunks,)),
            dma((n_chunks,)),
            dma((n_chunks, m - 1)),
            dma((n_chunks, m - 1)),
            dma((n_chunks, m - 1)),
            dma((n_chunks, m - 1)),
            dma((2, n_chunks, n_ch - 1)),
            dma((2, n_chunks, n_ch - 1)),
            dma((2, n_chunks)),
            dma((2, n_chunks)),
            dma((n_chunks, m - 1)),
            dma((n_chunks, m - 1)),
            dma((n_chunks, 2)),
            dma((n_chunks, 2)),
            dma((n_chunks, 2)),
            dma((n_chunks,)),
        ],
        compiler_params=pltpu.CompilerParams(
            collective_id=0, has_side_effects=True, vmem_limit_bytes=62 * 2**20
        ),
        name="admm",
    )(vis, model, stations, initial_gains, basis)
    step = n_dir // FINISH_STEPS
    whole = pl.BlockSpec((2, step) + initial_gains.shape[2:], lambda i: (0, i, 0, 0))
    return pl.pallas_call(
        functools.partial(finish_kernel, ns),
        grid=(FINISH_STEPS,),
        out_shape=(out, out),
        in_specs=[
            whole,
            pl.BlockSpec((step,) + fits.shape[1:], lambda i: (i, 0, 0)),
            pl.BlockSpec(basis.shape, lambda i: (0, 0, 0, 0)),
        ],
        out_specs=(whole, whole),
        compiler_params=pltpu.CompilerParams(vmem_limit_bytes=62 * 2**20),
        name="finish",
    )(gains, coefs, basis)


def solution(mesh):
    placed = (
        P(None, "ch", "bl"),
        P(None, None, "ch", "bl"),
        P(None, "bl"),
        P(None, None, "ch", None),
    )
    return jax.shard_map(
        functools.partial(per_device, mesh.shape["bl"], mesh.shape["ch"]),
        mesh=mesh,
        in_specs=placed,
        out_specs=(P(None, None, "ch", None), P(None, None, "ch", None)),
        check_vma=False,
    )
```

```python
import functools

import jax
import jax.numpy as jnp
import numpy as np
from jax import lax
from jax.experimental import pallas as pl
from jax.experimental.pallas import tpu as pltpu
from jax.sharding import PartitionSpec as P

SPECTRAL_BINS = 64
ITERS = 3
penalty = 1.0
MESH = pl.DeviceIdType.MESH
BLOCK = 512
CH = 8
FINISH_STEPS = 2
ORDER = (("A", 0), ("F", 0), ("F", 1), ("A", 1), ("U", 0), ("U", 1), ("B", 0), ("B", 1))


def legendre_basis(channel_count):
    steps = np.arange(channel_count, dtype=np.float32)
    abscissa = np.float32(-1.0) + np.float32(2.0) * steps / np.float32(channel_count - 1)
    columns = []
    for degree in range(4):
        vector = abscissa**degree
        for earlier in columns:
            vector = vector - np.sum(earlier * vector) * earlier
        vector = vector / np.sqrt(np.sum(vector * vector))
        columns.append(vector.astype(np.float32))
    return np.stack(columns, axis=1)


def split(value):
    high = value.astype(jnp.bfloat16)
    return high, (value - high.astype(jnp.float32)).astype(jnp.bfloat16)


def swap_halves(first, second, groups):
    if groups == 1:
        return [first]
    half = CH // 2
    return [
        jnp.concatenate([first[:half], second[:half]], axis=0),
        jnp.concatenate([first[half:], second[half:]], axis=0),
    ]


def admm_kernel(
    cfg, vis_hbm, model_hbm, ids_hbm, init_hbm, basis_hbm, out_g, cfull,
    vbuf, vgrp, mbuf, ibuf, hot, hot_t, pieces, gbuf, res, tacc, acc, rsbuf, ginit, gains,
    cons, dual, shif, basis, cpart, zbuf, zsum, sbuf, ctot,
    ld_sem, m_load, x_send, x_recv, m_send, m_recv, rs_send, rs_recv, ag_send, ag_recv,
    z_send, z_recv, s_send, s_recv, k_send, k_recv, o_send, o_recv, g_sem, c_sem,
):
    ns, m, n_ch, n_dir, n_base, groups, e = cfg
    n_st = init_hbm.shape[3]
    me = lax.axis_index("bl")
    ch = lax.axis_index("ch")
    core = lax.rem(me, ns)
    gi = me // ns
    sib = (me + 1 - 2 * core, ch)
    units = n_dir // groups
    per = m * e
    n_c = units // per
    sub = CH // groups
    nbs = n_base // BLOCK
    n_blk = ns * nbs
    steps = ITERS * groups

    def peer(t):
        return (lax.rem(gi + t, m) * ns + core, ch)

    def zpeer(t):
        return (me, lax.rem(ch + t, n_ch))

    others = [peer(t) for t in range(1, m)] + [zpeer(t) for t in range(1, n_ch)]
    if ns == 2:
        others.append(sib)
    barrier = pltpu.get_barrier_semaphore()
    for dev in others:
        pl.semaphore_signal(barrier, inc=1, device_id=dev, device_id_type=MESH)

    own = pl.ds(pl.multiple_of(core * CH, CH), CH)
    theirs = pl.ds(pl.multiple_of((ns - 1 - core) * CH, CH), CH)
    loads = [
        pltpu.make_async_copy(ids_hbm, ibuf.at[core], ld_sem.at[0]),
        pltpu.make_async_copy(init_hbm.at[0, :, own], ginit.at[:, 0], ld_sem.at[1]),
        pltpu.make_async_copy(init_hbm.at[1, :, own], ginit.at[:, 1], ld_sem.at[2]),
        pltpu.make_async_copy(vis_hbm.at[:, own], vbuf.at[core], ld_sem.at[3]),
        pltpu.make_async_copy(
            basis_hbm.at[pl.ds((ch * ns + core) * groups, groups)], basis, ld_sem.at[4]
        ),
    ]
    for copy in loads:
        copy.start()

    def model_load(c):
        dirs = pl.ds(c * per * groups, per * groups)
        return pltpu.make_async_copy(
            model_hbm.at[:, dirs, own], mbuf.at[core, :, dirs], m_load.at[c]
        )

    for c in range(n_c):
        model_load(c).start()

    def remote(src, dst, send, recv, dev):
        return pltpu.make_async_remote_copy(
            src_ref=src, dst_ref=dst, send_sem=send, recv_sem=recv,
            device_id=dev, device_id_type=MESH,
        )

    def model_swap(c):
        dirs = pl.ds(c * per * groups, per * groups)
        return remote(
            model_hbm.at[:, dirs, theirs], mbuf.at[core, :, dirs], m_send.at[c], m_recv.at[c], sib
        )

    def build(src):
        def body(b, _):
            for side in range(2):
                row = ibuf[src, pl.ds(side, 1), pl.ds(pl.multiple_of(b * BLOCK, BLOCK), BLOCK)]
                station = lax.broadcasted_iota(jnp.int32, (n_st, BLOCK), 0)
                one = (station == row).astype(jnp.float32).astype(jnp.bfloat16)
                hot[src * nbs + b, :, pl.ds(side * BLOCK, BLOCK)] = one
            return 0

        lax.fori_loop(0, nbs, body, 0, unroll=nbs)

    def build_t(src):
        def body(b, _):
            for side in range(2):
                row = ibuf[src, pl.ds(side, 1), pl.ds(pl.multiple_of(b * BLOCK, BLOCK), BLOCK)]
                for i in range(BLOCK // 128):
                    col = jnp.transpose(
                        jnp.broadcast_to(row[:, i * 128 : (i + 1) * 128], (128, 128))
                    )
                    lane = lax.broadcasted_iota(jnp.int32, (128, 128), 1)
                    for j in range(n_st // 128):
                        one = (col == lane + j * 128).astype(jnp.float32).astype(jnp.bfloat16)
                        where = pl.ds(side * BLOCK + i * 128, 128)
                        hot_t[src * nbs + b, where, pl.ds(j * 128, 128)] = one
            return 0

        lax.fori_loop(0, nbs, body, 0, unroll=nbs)

    loads[0].wait()
    build(core)
    pl.semaphore_wait(barrier, len(others))
    swaps = []
    if ns == 2:
        swaps = [
            remote(ibuf.at[core], ibuf.at[core], x_send.at[0], x_recv.at[0], sib),
            remote(vis_hbm.at[:, theirs], vbuf.at[core], x_send.at[1], x_recv.at[1], sib),
        ]
        for copy in swaps:
            copy.start()
        for c in range(n_c):
            model_swap(c).start()
    build_t(core)
    if ns == 2:
        swaps[0].wait_recv()
        build(1 - core)
        build_t(1 - core)
    for copy in loads[1:]:
        copy.wait()
    for copy in swaps[1:]:
        copy.wait_recv()

    for u in range(units):
        for part in range(2):
            first = ginit[u * groups, part]
            second = ginit[u * groups + groups - 1, part]
            for g, tile in enumerate(swap_halves(first, second, groups)):
                gains[g, u, part] = tile
    for b in range(n_blk):
        src, lanes = b // nbs, pl.ds((b % nbs) * BLOCK, BLOCK)
        for part in range(2):
            tile = vbuf[src, part, :, lanes]
            for g, both in enumerate(swap_halves(tile, tile, groups)):
                vgrp[g, b, part] = both
    for g in range(groups):
        for c in range(n_c):
            for i in range(e):
                cons[g * n_c + c, i] = gains[g, c * per + gi * e + i]
    dual[...] = jnp.zeros_like(dual)

    def own_units(c):
        return pl.ds(c * per + gi * e, e)

    def rs_copy(g, c, t):
        k = g * n_c + c
        return remote(
            acc.at[k, pl.ds(lax.rem(gi + t, m) * e, e)], rsbuf.at[k, t - 1],
            rs_send.at[k, t - 1], rs_recv.at[k, t - 1], peer(t),
        )

    def ag_copy(g, c, t):
        k = g * n_c + c
        return remote(
            gains.at[g, own_units(c)], gains.at[g, own_units(c)],
            ag_send.at[k, t - 1], ag_recv.at[k, t - 1], peer(t),
        )

    def z_copy(par, c, t):
        return remote(
            cpart.at[par, c], zbuf.at[par, c, t - 1],
            z_send.at[par, c, t - 1], z_recv.at[par, c, t - 1], zpeer(t),
        )

    def s_copy(par, c):
        return remote(
            zsum.at[par, c], sbuf.at[par, c], s_send.at[par, c], s_recv.at[par, c], sib
        )

    def k_copy(c, t):
        return remote(
            ctot.at[c], cfull.at[own_units(c)], k_send.at[c, t - 1], k_recv.at[c, t - 1], peer(t)
        )

    def arrange(c):
        if groups == 1:
            return

        def body(i, _):
            src = i // (2 * per)
            part = lax.rem(i // per, 2)
            slot = (c * per + lax.rem(i, per)) * groups
            tiles = swap_halves(mbuf[src, part, slot], mbuf[src, part, slot + 1], groups)
            mbuf[src, part, slot] = tiles[0]
            mbuf[src, part, slot + 1] = tiles[1]
            return 0

        lax.fori_loop(0, ns * 2 * per, body, 0, unroll=4)

    def gather_chunk(g, c):
        for i in range(per):
            high, low = split(gains[g, c * per + i].reshape(2 * CH, n_st))
            pieces[pl.ds(i * 2 * CH, 2 * CH), :] = high
            pieces[pl.ds((per + i) * 2 * CH, 2 * CH), :] = low

        def body(b, _):
            src = b // nbs
            lanes = pl.ds(pl.multiple_of(lax.rem(b, nbs) * BLOCK, BLOCK), BLOCK)
            both = jnp.dot(pieces[...], hot[b], preferred_element_type=jnp.float32)
            half = per * 2 * CH
            res_re = res[b, 0]
            res_im = res[b, 1]
            for i in range(per):
                u = c * per + i
                d = u * groups + g
                lo = i * 2 * CH
                value = both[lo : lo + 2 * CH] + both[half + lo : half + lo + 2 * CH]
                gbuf[u, b] = value
                l_re, l_im = value[:CH, :BLOCK], value[CH:, :BLOCK]
                r_re, r_im = value[:CH, BLOCK:], value[CH:, BLOCK:]
                m_re, m_im = mbuf[src, 0, d, :, lanes], mbuf[src, 1, d, :, lanes]
                a_re = m_re * r_re + m_im * r_im
                a_im = m_im * r_re - m_re * r_im
                res_re = res_re - (l_re * a_re - l_im * a_im)
                res_im = res_im - (l_re * a_im + l_im * a_re)
            res[b, 0] = res_re
            res[b, 1] = res_im
            return 0

        lax.fori_loop(0, n_blk, body, 0, unroll=n_blk)

    def fold(value):
        if groups == 1:
            return value
        return value + jnp.concatenate([value[sub:], value[:sub]], axis=0)

    def scatter_chunk(g, c):
        tacc[...] = jnp.zeros_like(tacc)

        def body(b, _):
            src = b // nbs
            lanes = pl.ds(pl.multiple_of(lax.rem(b, nbs) * BLOCK, BLOCK), BLOCK)
            res_re = vgrp[g, b, 0] + fold(res[b, 0])
            res_im = vgrp[g, b, 1] + fold(res[b, 1])
            sides = [[], []]
            for i in range(per):
                u = c * per + i
                d = u * groups + g
                m_re, m_im = mbuf[src, 0, d, :, lanes], mbuf[src, 1, d, :, lanes]
                t_re = res_re * m_re + res_im * m_im
                t_im = res_re * m_im - res_im * m_re
                power = m_re * m_re + m_im * m_im
                for side in range(2):
                    other = pl.ds((1 - side) * BLOCK, BLOCK)
                    g_re = gbuf[u, b, pl.ds(0, CH), other]
                    g_im = gbuf[u, b, pl.ds(CH, CH), other]
                    if side == 0:
                        re = t_re * g_re + t_im * g_im
                        im = t_re * g_im - t_im * g_re
                    else:
                        re = t_re * g_re - t_im * g_im
                        im = t_re * g_im + t_im * g_re
                    w = power * (g_re * g_re + g_im * g_im)
                    sides[side].append((re, im, w))
            parts = []
            for side in range(2):
                num_h, num_l = [], []
                for re, im, _w in sides[side]:
                    high, low = split(jnp.concatenate([re, im], axis=0))
                    num_h.append(high)
                    num_l.append(low)
                for i in range(0, per, 2):
                    pair = [sides[side][i][2], sides[side][i + 1][2]]
                    high, low = split(jnp.concatenate(pair, axis=0))
                    num_h.append(high)
                    num_l.append(low)
                parts.append(jnp.concatenate(num_h + num_l, axis=0))
            terms = jnp.concatenate(parts, axis=1)
            tacc[...] += jnp.dot(terms, hot_t[b], preferred_element_type=jnp.float32)
            return 0

        lax.fori_loop(0, n_blk, body, 0, unroll=n_blk)
        half = per * 3 * CH
        k = g * n_c + c
        for i in range(per):
            a, w = i * 2 * CH, per * 2 * CH + i * CH
            acc[k, i, pl.ds(0, 2 * CH), :] = (
                tacc[pl.ds(a, 2 * CH), :] + tacc[pl.ds(half + a, 2 * CH), :]
            )
            acc[k, i, pl.ds(2 * CH, CH), :] = (
                tacc[pl.ds(w, CH), :] + tacc[pl.ds(half + w, CH), :]
            )
        for t in range(1, m):
            rs_copy(g, c, t).start()

    def wide(g, degree):
        return jnp.concatenate([basis[g, degree]] * (n_st // 128), axis=1)

    def fit_sum(par, c):
        for t in range(1, n_ch):
            z_copy(par, c, t).wait_recv()
        value = cpart[par, c]
        for t in range(1, n_ch):
            value = value + zbuf[par, c, t - 1]
        zsum[par, c] = value
        if ns == 2:
            s_copy(par, c).start()
        for t in range(1, n_ch):
            z_copy(par, c, t).wait_send()

    def fit_total(par, c):
        value = zsum[par, c]
        if ns == 2:
            s_copy(par, c).wait_recv()
            value = value + sbuf[par, c]
            s_copy(par, c).wait_send()
        ctot[c] = value

    def fit(g, c):
        k = g * n_c + c
        for i in range(e):
            for part in range(2):
                line = None
                for degree in range(4):
                    rows = [
                        jnp.broadcast_to(
                            ctot[c, i, pl.ds(j * 8 + degree * 2 + part, 1)], (sub, n_st)
                        )
                        for j in range(groups)
                    ]
                    term = wide(g, degree) * jnp.concatenate(rows, axis=0)
                    line = term if line is None else line + term
                cons[k, i, part] = line
                dual[k, i, part] = shif[k, i, part] - line

    def update(s, c):
        it = s // groups
        g = lax.rem(s, groups)
        par = lax.rem(it, 2)
        k = g * n_c + c
        for t in range(1, m):
            rs_copy(g, c, t).wait_recv()

        @pl.when(it > 0)
        def _():
            for t in range(1, m):
                ag_copy(g, c, t).wait_send()

            @pl.when(g == 0)
            def _():
                fit_total(1 - par, c)

            fit(g, c)

        for i in range(e):
            u = c * per + gi * e + i
            total = acc[k, gi * e + i]
            for t in range(1, m):
                total = total + rsbuf[k, t - 1, i]
            weight = total[2 * CH :]
            factor = 1.0 / (weight + penalty)
            for part in range(2):
                num = total[part * CH : (part + 1) * CH] + gains[g, u, part] * weight
                new = (num + penalty * (cons[k, i, part] - dual[k, i, part])) * factor
                gains[g, u, part] = new
                shif[k, i, part] = new + dual[k, i, part]
        for t in range(1, m):
            ag_copy(g, c, t).start()
        for i in range(e):
            rows = [None] * (8 * groups)
            for part in range(2):
                for degree in range(4):
                    line = shif[k, i, part] * wide(g, degree)
                    for j in range(groups):
                        rows[j * 8 + degree * 2 + part] = jnp.sum(
                            line[j * sub : (j + 1) * sub], axis=0, keepdims=True
                        )
            block = jnp.concatenate(rows, axis=0)
            if groups == 1:
                cpart[par, c, i] = block
            else:

                @pl.when(g == 0)
                def _(i=i, block=block):
                    cpart[par, c, i] = block

                @pl.when(g > 0)
                def _(i=i, block=block):
                    cpart[par, c, i] = cpart[par, c, i] + block

        @pl.when(g == groups - 1)
        def _():
            for t in range(1, n_ch):
                z_copy(par, c, t).start()

        for t in range(1, m):
            rs_copy(g, c, t).wait_send()

    def step(s, _):
        it = s // groups
        g = lax.rem(s, groups)
        res[...] = jnp.zeros_like(res)

        def gather_step(c, _):
            @pl.when(it > 0)
            def _():
                for t in range(1, m):
                    ag_copy(g, c, t).wait_recv()

            @pl.when(s == 0)
            def _():
                model_load(c).wait()
                if ns == 2:
                    model_swap(c).wait_recv()
                arrange(c)

            gather_chunk(g, c)
            return 0

        def sum_step(c):
            @pl.when((it > 0) & (g == groups - 1))
            def _():
                fit_sum(lax.rem(it + 1, 2), c)

        def update_step(c):
            @pl.when(s > 0)
            def _():
                update(s - 1, c)

        if groups > 1:
            act = {"A": lambda c: gather_step(c, 0), "B": lambda c: scatter_chunk(g, c),
                   "U": update_step, "F": sum_step}
            for name, c in ORDER:
                act[name](c)
        else:
            lax.fori_loop(0, n_c, gather_step, 0)
            for c in range(n_c):
                scatter_chunk(g, c)

            @pl.when(it > 0)
            def _():
                for c in range(n_c):
                    fit_sum(lax.rem(it + 1, 2), c)

            for c in range(n_c):
                update(s, c)
        return 0

    lax.fori_loop(0, steps, step, 0)

    par = (ITERS - 1) % 2
    if groups > 1:
        for c in range(n_c):
            update(steps - 1, c)

    def o_copy(g, c, part):
        where = pl.ds(c * per, per)
        return remote(
            gains.at[g, where, part], out_g.at[part, g, where, own],
            o_send.at[g, c, part], o_recv.at[g, c, part], sib,
        )

    def g_copy(g, c, part):
        where = pl.ds(c * per, per)
        return pltpu.make_async_copy(
            gains.at[g, where, part], out_g.at[part, g, where, own], g_sem.at[g, c, part]
        )

    def c_copy(c):
        return pltpu.make_async_copy(ctot.at[c], cfull.at[own_units(c)], c_sem.at[c])

    def give_gains(g, c):
        for t in range(1, m):
            ag_copy(g, c, t).wait_recv()
        for part in range(2):
            if ns == 2:
                o_copy(g, c, part).start()
            g_copy(g, c, part).start()

    for g in range(groups - 1):
        for c in range(n_c):
            give_gains(g, c)
    for c in range(n_c):
        fit_sum(par, c)
    for c in range(n_c):
        fit_total(par, c)
        c_copy(c).start()
        for t in range(1, m):
            k_copy(c, t).start()
    for c in range(n_c):
        give_gains(groups - 1, c)
    for c in range(n_c):
        c_copy(c).wait()
        for t in range(1, m):
            k_copy(c, t).wait_recv()
            k_copy(c, t).wait_send()
        if ns == 2:
            model_swap(c).wait_send()
        for g in range(groups):
            for t in range(1, m):
                ag_copy(g, c, t).wait_send()
            for part in range(2):
                g_copy(g, c, part).wait()
                if ns == 2:
                    o_copy(g, c, part).wait_recv()
                    o_copy(g, c, part).wait_send()
    for copy in swaps:
        copy.wait_send()


def finish_kernel(ns, groups, gains_ref, coef_ref, basis_ref, out_g, out_c):
    n_dir, _, n_st = coef_ref.shape
    ch = lax.axis_index("ch")
    for h in range(ns):
        rows = pl.ds(h * CH, CH)
        for u in range(n_dir // groups):
            for part in range(2):
                first = gains_ref[part, 0, u, rows, :]
                second = gains_ref[part, groups - 1, u, rows, :]
                for j, tile in enumerate(swap_halves(first, second, groups)):
                    out_g[part, u * groups + j, rows, :] = tile
        base = [
            jnp.concatenate([basis_ref[ch * ns + h, k]] * (n_st // 128), axis=1) for k in range(4)
        ]
        for d in range(n_dir):
            for part in range(2):
                line = base[0] * coef_ref[d, pl.ds(part, 1)]
                for k in range(1, 4):
                    line = line + base[k] * coef_ref[d, pl.ds(2 * k + part, 1)]
                out_c[part, d, rows, :] = line


def per_device(n, n_ch, vis, model, stations, initial_gains):
    n_dir, n_chan, n_st = initial_gains.shape[1:]
    n_base = model.shape[3]
    ns = n_chan // CH
    m = n // ns
    groups = 2 if n_dir % (4 * m) == 0 else 1
    units = n_dir // groups
    e = max(1, units // (2 * m)) if groups == 2 else units // m
    per = m * e
    n_c = units // per
    k_all = groups * n_c
    n_blk = ns * n_base // BLOCK
    sub = CH // groups
    table = legendre_basis(SPECTRAL_BINS).reshape(SPECTRAL_BINS // CH, CH, 4).transpose(0, 2, 1)
    tiled = table.reshape(SPECTRAL_BINS // CH, 4, groups, 1, sub).transpose(0, 2, 1, 3, 4)
    tiled = np.broadcast_to(tiled, tiled.shape[:3] + (groups, sub)).reshape(-1, 4, CH)

    def spread(rows):
        return jnp.asarray(np.ascontiguousarray(np.broadcast_to(rows[..., None], rows.shape + (128,))))

    basis, unit_basis = spread(table), spread(tiled)
    f32, bf16 = jnp.float32, jnp.bfloat16
    dma = pltpu.SemaphoreType.DMA
    hbm = pl.BlockSpec(memory_space=pl.ANY)
    out = jax.ShapeDtypeStruct(initial_gains.shape, f32)
    mixed = jax.ShapeDtypeStruct((2, groups, units, n_chan, n_st), f32)
    fits = jax.ShapeDtypeStruct((units, 8 * groups, n_st), f32)
    gains, coefs = pl.pallas_call(
        functools.partial(admm_kernel, (ns, m, n_ch, n_dir, n_base, groups, e)),
        out_shape=(mixed, fits),
        in_specs=[hbm, hbm, hbm, hbm, hbm],
        out_specs=(hbm, hbm),
        scratch_shapes=[
            pltpu.VMEM((ns, 2, CH, n_base), f32),
            pltpu.VMEM((groups, n_blk, 2, CH, BLOCK), f32),
            pltpu.VMEM((ns, 2, n_dir, CH, n_base), f32),
            pltpu.VMEM((ns, 2, n_base), jnp.int32),
            pltpu.VMEM((n_blk, n_st, 2 * BLOCK), bf16),
            pltpu.VMEM((n_blk, 2 * BLOCK, n_st), bf16),
            pltpu.VMEM((4 * per * CH, n_st), bf16),
            pltpu.VMEM((units, n_blk, 2 * CH, 2 * BLOCK), f32),
            pltpu.VMEM((n_blk, 2, CH, BLOCK), f32),
            pltpu.VMEM((6 * per * CH, n_st), f32),
            pltpu.VMEM((k_all, per, 3 * CH, n_st), f32),
            pltpu.VMEM((k_all, m - 1, e, 3 * CH, n_st), f32),
            pltpu.VMEM((n_dir, 2, CH, n_st), f32),
            pltpu.VMEM((groups, units, 2, CH, n_st), f32),
            pltpu.VMEM((k_all, e, 2, CH, n_st), f32),
            pltpu.VMEM((k_all, e, 2, CH, n_st), f32),
            pltpu.VMEM((k_all, e, 2, CH, n_st), f32),
            pltpu.VMEM((groups, 4, CH, 128), f32),
            pltpu.VMEM((2, n_c, e, 8 * groups, n_st), f32),
            pltpu.VMEM((2, n_c, n_ch - 1, e, 8 * groups, n_st), f32),
            pltpu.VMEM((2, n_c, e, 8 * groups, n_st), f32),
            pltpu.VMEM((2, n_c, e, 8 * groups, n_st), f32),
            pltpu.VMEM((n_c, e, 8 * groups, n_st), f32),
            dma((5,)),
            dma((n_c,)),
            dma((2,)),
            dma((2,)),
            dma((n_c,)),
            dma((n_c,)),
            dma((k_all, m - 1)),
            dma((k_all, m - 1)),
            dma((k_all, m - 1)),
            dma((k_all, m - 1)),
            dma((2, n_c, n_ch - 1)),
            dma((2, n_c, n_ch - 1)),
            dma((2, n_c)),
            dma((2, n_c)),
            dma((n_c, m - 1)),
            dma((n_c, m - 1)),
            dma((groups, n_c, 2)),
            dma((groups, n_c, 2)),
            dma((groups, n_c, 2)),
            dma((n_c,)),
        ],
        compiler_params=pltpu.CompilerParams(
            collective_id=0, has_side_effects=True, vmem_limit_bytes=62 * 2**20
        ),
        name="admm",
    )(vis, model, stations, initial_gains, unit_basis)
    coefs = coefs.reshape(n_dir, 8, n_st)
    block = n_dir // FINISH_STEPS
    whole = pl.BlockSpec((2, block, n_chan, n_st), lambda i: (0, i, 0, 0))
    return pl.pallas_call(
        functools.partial(finish_kernel, ns, groups),
        grid=(FINISH_STEPS,),
        out_shape=(out, out),
        in_specs=[
            pl.BlockSpec((2, groups, block // groups, n_chan, n_st), lambda i: (0, 0, i, 0, 0)),
            pl.BlockSpec((block, 8, n_st), lambda i: (i, 0, 0)),
            pl.BlockSpec(basis.shape, lambda i: (0, 0, 0, 0)),
        ],
        out_specs=(whole, whole),
        compiler_params=pltpu.CompilerParams(vmem_limit_bytes=62 * 2**20),
        name="finish",
    )(gains, coefs, basis)


def solution(mesh):
    placed = (
        P(None, "ch", "bl"),
        P(None, None, "ch", "bl"),
        P(None, "bl"),
        P(None, None, "ch", None),
    )
    return jax.shard_map(
        functools.partial(per_device, mesh.shape["bl"], mesh.shape["ch"]),
        mesh=mesh,
        in_specs=placed,
        out_specs=(P(None, None, "ch", None), P(None, None, "ch", None)),
        check_vma=False,
    )
```

```python
import functools

import jax
import jax.numpy as jnp
import numpy as np
from jax import lax
from jax.experimental import pallas as pl
from jax.experimental.pallas import tpu as pltpu
from jax.sharding import PartitionSpec as P

SPECTRAL_BINS = 64
ITERS = 3
penalty = 1.0
MESH = pl.DeviceIdType.MESH
BLOCK = 512
CH = 8
FINISH_STEPS = 2
ORDER = (
    ("A", 0), ("F", 0), ("F", 1), ("A", 1), ("U", 0), ("R", 0), ("U", 1), ("R", 1), ("B", 0), ("B", 1),
)


def legendre_basis(channel_count):
    steps = np.arange(channel_count, dtype=np.float32)
    abscissa = np.float32(-1.0) + np.float32(2.0) * steps / np.float32(channel_count - 1)
    columns = []
    for degree in range(4):
        vector = abscissa**degree
        for earlier in columns:
            vector = vector - np.sum(earlier * vector) * earlier
        vector = vector / np.sqrt(np.sum(vector * vector))
        columns.append(vector.astype(np.float32))
    return np.stack(columns, axis=1)


def split(value):
    high = value.astype(jnp.bfloat16)
    return high, (value - high.astype(jnp.float32)).astype(jnp.bfloat16)


def swap_halves(first, second, groups):
    if groups == 1:
        return [first]
    half = CH // 2
    return [
        jnp.concatenate([first[:half], second[:half]], axis=0),
        jnp.concatenate([first[half:], second[half:]], axis=0),
    ]


def admm_kernel(
    cfg, vis_hbm, model_hbm, ids_hbm, init_hbm, basis_hbm, out_g, cfull,
    vbuf, vgrp, mbuf, ibuf, hot, hot_t, pieces, gbuf, res, tacc, acc, rsbuf, ginit, gains,
    cons, dual, shif, basis, cpart, zbuf, zsum, sbuf, ctot,
    ld_sem, m_load, x_send, x_recv, m_send, m_recv, rs_send, rs_recv, ag_send, ag_recv,
    z_send, z_recv, s_send, s_recv, k_send, k_recv, o_send, o_recv, g_sem, c_sem,
):
    ns, m, n_ch, n_dir, n_base, groups, e = cfg
    n_st = init_hbm.shape[3]
    me = lax.axis_index("bl")
    ch = lax.axis_index("ch")
    core = lax.rem(me, ns)
    gi = me // ns
    sib = (me + 1 - 2 * core, ch)
    units = n_dir // groups
    per = m * e
    n_c = units // per
    sub = CH // groups
    nbs = n_base // BLOCK
    n_blk = ns * nbs
    steps = ITERS * groups

    def peer(t):
        return (lax.rem(gi + t, m) * ns + core, ch)

    def zpeer(t):
        return (me, lax.rem(ch + t, n_ch))

    others = [peer(t) for t in range(1, m)] + [zpeer(t) for t in range(1, n_ch)]
    if ns == 2:
        others.append(sib)
    barrier = pltpu.get_barrier_semaphore()
    for dev in others:
        pl.semaphore_signal(barrier, inc=1, device_id=dev, device_id_type=MESH)

    own = pl.ds(pl.multiple_of(core * CH, CH), CH)
    theirs = pl.ds(pl.multiple_of((ns - 1 - core) * CH, CH), CH)
    loads = [
        pltpu.make_async_copy(ids_hbm, ibuf.at[core], ld_sem.at[0]),
        pltpu.make_async_copy(init_hbm.at[0, :, own], ginit.at[:, 0], ld_sem.at[1]),
        pltpu.make_async_copy(init_hbm.at[1, :, own], ginit.at[:, 1], ld_sem.at[2]),
        pltpu.make_async_copy(vis_hbm.at[:, own], vbuf.at[core], ld_sem.at[3]),
        pltpu.make_async_copy(
            basis_hbm.at[pl.ds((ch * ns + core) * groups, groups)], basis, ld_sem.at[4]
        ),
    ]
    for copy in loads:
        copy.start()

    def model_load(c):
        dirs = pl.ds(c * per * groups, per * groups)
        return pltpu.make_async_copy(
            model_hbm.at[:, dirs, own], mbuf.at[core, :, dirs], m_load.at[c]
        )

    for c in range(n_c):
        model_load(c).start()

    def remote(src, dst, send, recv, dev):
        return pltpu.make_async_remote_copy(
            src_ref=src, dst_ref=dst, send_sem=send, recv_sem=recv,
            device_id=dev, device_id_type=MESH,
        )

    def model_swap(c):
        dirs = pl.ds(c * per * groups, per * groups)
        return remote(
            model_hbm.at[:, dirs, theirs], mbuf.at[core, :, dirs], m_send.at[c], m_recv.at[c], sib
        )

    def build(src):
        def body(b, _):
            for side in range(2):
                row = ibuf[src, pl.ds(side, 1), pl.ds(pl.multiple_of(b * BLOCK, BLOCK), BLOCK)]
                station = lax.broadcasted_iota(jnp.int32, (n_st, BLOCK), 0)
                one = (station == row).astype(jnp.float32).astype(jnp.bfloat16)
                hot[src * nbs + b, :, pl.ds(side * BLOCK, BLOCK)] = one
            return 0

        lax.fori_loop(0, nbs, body, 0, unroll=nbs)

    def build_t(src):
        def body(b, _):
            for side in range(2):
                row = ibuf[src, pl.ds(side, 1), pl.ds(pl.multiple_of(b * BLOCK, BLOCK), BLOCK)]
                for i in range(BLOCK // 128):
                    col = jnp.transpose(
                        jnp.broadcast_to(row[:, i * 128 : (i + 1) * 128], (128, 128))
                    )
                    lane = lax.broadcasted_iota(jnp.int32, (128, 128), 1)
                    for j in range(n_st // 128):
                        one = (col == lane + j * 128).astype(jnp.float32).astype(jnp.bfloat16)
                        where = pl.ds(side * BLOCK + i * 128, 128)
                        hot_t[src * nbs + b, where, pl.ds(j * 128, 128)] = one
            return 0

        lax.fori_loop(0, nbs, body, 0, unroll=nbs)

    def own_units(c):
        return pl.ds(c * per + gi * e, e)

    def rs_copy(g, c, t):
        k = g * n_c + c
        return remote(
            acc.at[k, pl.ds(lax.rem(gi + t, m) * e, e)], rsbuf.at[k, t - 1],
            rs_send.at[k, t - 1], rs_recv.at[k, t - 1], peer(t),
        )

    def ag_copy(g, c, t):
        k = g * n_c + c
        return remote(
            gains.at[g, own_units(c)], gains.at[g, own_units(c)],
            ag_send.at[k, t - 1], ag_recv.at[k, t - 1], peer(t),
        )

    def z_copy(par, c, t):
        return remote(
            cpart.at[par, c], zbuf.at[par, c, t - 1],
            z_send.at[par, c, t - 1], z_recv.at[par, c, t - 1], zpeer(t),
        )

    def s_copy(par, c):
        return remote(
            zsum.at[par, c], sbuf.at[par, c], s_send.at[par, c], s_recv.at[par, c], sib
        )

    def k_copy(c, t):
        return remote(
            ctot.at[c], cfull.at[own_units(c)], k_send.at[c, t - 1], k_recv.at[c, t - 1], peer(t)
        )

    def arrange(src, c):
        if groups == 1:
            return

        def body(i, _):
            part = i // per
            slot = (c * per + lax.rem(i, per)) * groups
            tiles = swap_halves(mbuf[src, part, slot], mbuf[src, part, slot + 1], groups)
            mbuf[src, part, slot] = tiles[0]
            mbuf[src, part, slot + 1] = tiles[1]
            return 0

        lax.fori_loop(0, 2 * per, body, 0, unroll=2 * per)

    def gather_chunk(g, c, first, count):
        for i in range(per):
            high, low = split(gains[g, c * per + i].reshape(2 * CH, n_st))
            pieces[pl.ds(i * 2 * CH, 2 * CH), :] = high
            pieces[pl.ds((per + i) * 2 * CH, 2 * CH), :] = low

        def body(j, _):
            b = first + j
            src = b // nbs
            lanes = pl.ds(pl.multiple_of(lax.rem(b, nbs) * BLOCK, BLOCK), BLOCK)
            both = jnp.dot(pieces[...], hot[b], preferred_element_type=jnp.float32)
            half = per * 2 * CH
            res_re = res[b, 0]
            res_im = res[b, 1]
            for i in range(per):
                u = c * per + i
                d = u * groups + g
                lo = i * 2 * CH
                value = both[lo : lo + 2 * CH] + both[half + lo : half + lo + 2 * CH]
                gbuf[u, b] = value
                l_re, l_im = value[:CH, :BLOCK], value[CH:, :BLOCK]
                r_re, r_im = value[:CH, BLOCK:], value[CH:, BLOCK:]
                m_re, m_im = mbuf[src, 0, d, :, lanes], mbuf[src, 1, d, :, lanes]
                a_re = m_re * r_re + m_im * r_im
                a_im = m_im * r_re - m_re * r_im
                res_re = res_re - (l_re * a_re - l_im * a_im)
                res_im = res_im - (l_re * a_im + l_im * a_re)
            res[b, 0] = res_re
            res[b, 1] = res_im
            return 0

        lax.fori_loop(0, count, body, 0, unroll=count)

    def fold(value):
        if groups == 1:
            return value
        return value + jnp.concatenate([value[sub:], value[:sub]], axis=0)

    def scatter_chunk(g, c):
        tacc[...] = jnp.zeros_like(tacc)

        def body(b, _):
            src = b // nbs
            lanes = pl.ds(pl.multiple_of(lax.rem(b, nbs) * BLOCK, BLOCK), BLOCK)
            res_re = vgrp[g, b, 0] + fold(res[b, 0])
            res_im = vgrp[g, b, 1] + fold(res[b, 1])
            sides = [[], []]
            for i in range(per):
                u = c * per + i
                d = u * groups + g
                m_re, m_im = mbuf[src, 0, d, :, lanes], mbuf[src, 1, d, :, lanes]
                t_re = res_re * m_re + res_im * m_im
                t_im = res_re * m_im - res_im * m_re
                power = m_re * m_re + m_im * m_im
                for side in range(2):
                    other = pl.ds((1 - side) * BLOCK, BLOCK)
                    g_re = gbuf[u, b, pl.ds(0, CH), other]
                    g_im = gbuf[u, b, pl.ds(CH, CH), other]
                    if side == 0:
                        re = t_re * g_re + t_im * g_im
                        im = t_re * g_im - t_im * g_re
                    else:
                        re = t_re * g_re - t_im * g_im
                        im = t_re * g_im + t_im * g_re
                    w = power * (g_re * g_re + g_im * g_im)
                    sides[side].append((re, im, w))
            parts = []
            for side in range(2):
                num_h, num_l = [], []
                for re, im, _w in sides[side]:
                    high, low = split(jnp.concatenate([re, im], axis=0))
                    num_h.append(high)
                    num_l.append(low)
                for i in range(0, per, 2):
                    pair = [sides[side][i][2], sides[side][i + 1][2]]
                    high, low = split(jnp.concatenate(pair, axis=0))
                    num_h.append(high)
                    num_l.append(low)
                parts.append(jnp.concatenate(num_h + num_l, axis=0))
            terms = jnp.concatenate(parts, axis=1)
            tacc[...] += jnp.dot(terms, hot_t[b], preferred_element_type=jnp.float32)
            return 0

        lax.fori_loop(0, n_blk, body, 0, unroll=n_blk)
        half = per * 3 * CH
        k = g * n_c + c
        for i in range(per):
            a, w = i * 2 * CH, per * 2 * CH + i * CH
            acc[k, i, pl.ds(0, 2 * CH), :] = (
                tacc[pl.ds(a, 2 * CH), :] + tacc[pl.ds(half + a, 2 * CH), :]
            )
            acc[k, i, pl.ds(2 * CH, CH), :] = (
                tacc[pl.ds(w, CH), :] + tacc[pl.ds(half + w, CH), :]
            )
        for t in range(1, m):
            rs_copy(g, c, t).start()

    def wide(g, degree):
        return jnp.concatenate([basis[g, degree]] * (n_st // 128), axis=1)

    def fit_sum(par, c):
        for t in range(1, n_ch):
            z_copy(par, c, t).wait_recv()
        value = cpart[par, c]
        for t in range(1, n_ch):
            value = value + zbuf[par, c, t - 1]
        zsum[par, c] = value
        if ns == 2:
            s_copy(par, c).start()
        for t in range(1, n_ch):
            z_copy(par, c, t).wait_send()

    def fit_total(par, c):
        value = zsum[par, c]
        if ns == 2:
            s_copy(par, c).wait_recv()
            value = value + sbuf[par, c]
            s_copy(par, c).wait_send()
        ctot[c] = value

    def fit(g, c):
        k = g * n_c + c
        for i in range(e):
            for part in range(2):
                line = None
                for degree in range(4):
                    rows = [
                        jnp.broadcast_to(
                            ctot[c, i, pl.ds(j * 8 + degree * 2 + part, 1)], (sub, n_st)
                        )
                        for j in range(groups)
                    ]
                    term = wide(g, degree) * jnp.concatenate(rows, axis=0)
                    line = term if line is None else line + term
                cons[k, i, part] = line
                dual[k, i, part] = shif[k, i, part] - line

    def update(s, c):
        it = s // groups
        g = lax.rem(s, groups)
        par = lax.rem(it, 2)
        k = g * n_c + c
        @pl.when(it > 0)
        def _():
            for t in range(1, m):
                ag_copy(g, c, t).wait_send()

            @pl.when(g == 0)
            def _():
                fit_total(1 - par, c)

            fit(g, c)

        for t in range(1, m):
            rs_copy(g, c, t).wait_recv()
        for i in range(e):
            u = c * per + gi * e + i
            total = acc[k, gi * e + i]
            for t in range(1, m):
                total = total + rsbuf[k, t - 1, i]
            weight = total[2 * CH :]
            factor = 1.0 / (weight + penalty)
            for part in range(2):
                num = total[part * CH : (part + 1) * CH] + gains[g, u, part] * weight
                new = (num + penalty * (cons[k, i, part] - dual[k, i, part])) * factor
                gains[g, u, part] = new
                shif[k, i, part] = new + dual[k, i, part]
        for t in range(1, m):
            ag_copy(g, c, t).start()

    def share(s, c):
        it = s // groups
        g = lax.rem(s, groups)
        par = lax.rem(it, 2)
        k = g * n_c + c
        for i in range(e):
            rows = [None] * (8 * groups)
            for part in range(2):
                for degree in range(4):
                    line = shif[k, i, part] * wide(g, degree)
                    for j in range(groups):
                        rows[j * 8 + degree * 2 + part] = jnp.sum(
                            line[j * sub : (j + 1) * sub], axis=0, keepdims=True
                        )
            block = jnp.concatenate(rows, axis=0)
            if groups == 1:
                cpart[par, c, i] = block
            else:

                @pl.when(g == 0)
                def _(i=i, block=block):
                    cpart[par, c, i] = block

                @pl.when(g > 0)
                def _(i=i, block=block):
                    cpart[par, c, i] = cpart[par, c, i] + block

        @pl.when(g == groups - 1)
        def _():
            for t in range(1, n_ch):
                z_copy(par, c, t).start()

        for t in range(1, m):
            rs_copy(g, c, t).wait_send()

    def step(s, _):
        it = s // groups
        g = lax.rem(s, groups)

        @pl.when(s > 0)
        def _():
            res[...] = jnp.zeros_like(res)

        def gather_step(c, _):
            @pl.when(it > 0)
            def _():
                for t in range(1, m):
                    ag_copy(g, c, t).wait_recv()

            @pl.when(s > 0)
            def _():
                gather_chunk(g, c, 0, n_blk)

            return 0

        def sum_step(c):
            @pl.when((it > 0) & (g == groups - 1))
            def _():
                fit_sum(lax.rem(it + 1, 2), c)

        def update_step(c):
            @pl.when(s > 0)
            def _():
                update(s - 1, c)

        def share_step(c):
            @pl.when(s > 0)
            def _():
                share(s - 1, c)

        if groups > 1:
            act = {"A": lambda c: gather_step(c, 0), "B": lambda c: scatter_chunk(g, c),
                   "U": update_step, "F": sum_step, "R": share_step}
            for name, c in ORDER:
                act[name](c)
        else:
            lax.fori_loop(0, n_c, gather_step, 0)
            for c in range(n_c):
                scatter_chunk(g, c)

            @pl.when(it > 0)
            def _():
                for c in range(n_c):
                    fit_sum(lax.rem(it + 1, 2), c)

            for c in range(n_c):
                update(s, c)
                share(s, c)
        return 0

    loads[0].wait()
    build(core)
    for copy in loads[1:]:
        copy.wait()
    for u in range(units):
        for part in range(2):
            first = ginit[u * groups, part]
            second = ginit[u * groups + groups - 1, part]
            for g, tile in enumerate(swap_halves(first, second, groups)):
                gains[g, u, part] = tile
    res[...] = jnp.zeros_like(res)

    def gather_part(src, c):
        arrange(src, c)
        gather_chunk(0, c, src * nbs, nbs)

    model_load(0).wait()
    gather_part(core, 0)
    pl.semaphore_wait(barrier, len(others))
    swaps = []
    if ns == 2:
        swaps = [
            remote(ibuf.at[core], ibuf.at[core], x_send.at[0], x_recv.at[0], sib),
            remote(vis_hbm.at[:, theirs], vbuf.at[core], x_send.at[1], x_recv.at[1], sib),
        ]
        for copy in swaps:
            copy.start()
        for c in range(n_c):
            model_swap(c).start()
    for c in range(1, n_c):
        model_load(c).wait()
        gather_part(core, c)
    build_t(core)
    for g in range(groups):
        for c in range(n_c):
            for i in range(e):
                cons[g * n_c + c, i] = gains[g, c * per + gi * e + i]
    dual[...] = jnp.zeros_like(dual)
    if ns == 2:
        swaps[0].wait_recv()
        build(1 - core)
        build_t(1 - core)
        swaps[1].wait_recv()
        for c in range(n_c):
            model_swap(c).wait_recv()
            gather_part(1 - core, c)
    for b in range(n_blk):
        src, lanes = b // nbs, pl.ds((b % nbs) * BLOCK, BLOCK)
        for part in range(2):
            tile = vbuf[src, part, :, lanes]
            for g, both in enumerate(swap_halves(tile, tile, groups)):
                vgrp[g, b, part] = both

    lax.fori_loop(0, steps, step, 0)

    par = (ITERS - 1) % 2
    if groups > 1:
        for c in range(n_c):
            update(steps - 1, c)
            share(steps - 1, c)

    def o_copy(g, c, part):
        where = pl.ds(c * per, per)
        return remote(
            gains.at[g, where, part], out_g.at[part, g, where, own],
            o_send.at[g, c, part], o_recv.at[g, c, part], sib,
        )

    def g_copy(g, c, part):
        where = pl.ds(c * per, per)
        return pltpu.make_async_copy(
            gains.at[g, where, part], out_g.at[part, g, where, own], g_sem.at[g, c, part]
        )

    def c_copy(c):
        return pltpu.make_async_copy(ctot.at[c], cfull.at[own_units(c)], c_sem.at[c])

    def give_gains(g, c):
        for t in range(1, m):
            ag_copy(g, c, t).wait_recv()
        for part in range(2):
            if ns == 2:
                o_copy(g, c, part).start()
            g_copy(g, c, part).start()

    for g in range(groups - 1):
        for c in range(n_c):
            give_gains(g, c)
    for c in range(n_c):
        fit_sum(par, c)
    for c in range(n_c):
        fit_total(par, c)
        c_copy(c).start()
        for t in range(1, m):
            k_copy(c, t).start()
    for c in range(n_c):
        give_gains(groups - 1, c)
    for c in range(n_c):
        c_copy(c).wait()
        for t in range(1, m):
            k_copy(c, t).wait_recv()
            k_copy(c, t).wait_send()
        if ns == 2:
            model_swap(c).wait_send()
        for g in range(groups):
            for t in range(1, m):
                ag_copy(g, c, t).wait_send()
            for part in range(2):
                g_copy(g, c, part).wait()
                if ns == 2:
                    o_copy(g, c, part).wait_recv()
                    o_copy(g, c, part).wait_send()
    for copy in swaps:
        copy.wait_send()


def finish_kernel(ns, groups, gains_ref, coef_ref, basis_ref, out_g, out_c):
    n_dir, _, n_st = coef_ref.shape
    ch = lax.axis_index("ch")
    for h in range(ns):
        rows = pl.ds(h * CH, CH)
        for u in range(n_dir // groups):
            for part in range(2):
                first = gains_ref[part, 0, u, rows, :]
                second = gains_ref[part, groups - 1, u, rows, :]
                for j, tile in enumerate(swap_halves(first, second, groups)):
                    out_g[part, u * groups + j, rows, :] = tile
        base = [
            jnp.concatenate([basis_ref[ch * ns + h, k]] * (n_st // 128), axis=1) for k in range(4)
        ]
        for d in range(n_dir):
            for part in range(2):
                line = base[0] * coef_ref[d, pl.ds(part, 1)]
                for k in range(1, 4):
                    line = line + base[k] * coef_ref[d, pl.ds(2 * k + part, 1)]
                out_c[part, d, rows, :] = line


def per_device(n, n_ch, vis, model, stations, initial_gains):
    n_dir, n_chan, n_st = initial_gains.shape[1:]
    n_base = model.shape[3]
    ns = n_chan // CH
    m = n // ns
    groups = 2 if n_dir % (4 * m) == 0 else 1
    units = n_dir // groups
    e = max(1, units // (2 * m)) if groups == 2 else units // m
    per = m * e
    n_c = units // per
    k_all = groups * n_c
    n_blk = ns * n_base // BLOCK
    sub = CH // groups
    table = legendre_basis(SPECTRAL_BINS).reshape(SPECTRAL_BINS // CH, CH, 4).transpose(0, 2, 1)
    tiled = table.reshape(SPECTRAL_BINS // CH, 4, groups, 1, sub).transpose(0, 2, 1, 3, 4)
    tiled = np.broadcast_to(tiled, tiled.shape[:3] + (groups, sub)).reshape(-1, 4, CH)

    def spread(rows):
        return jnp.asarray(np.ascontiguousarray(np.broadcast_to(rows[..., None], rows.shape + (128,))))

    basis, unit_basis = spread(table), spread(tiled)
    f32, bf16 = jnp.float32, jnp.bfloat16
    dma = pltpu.SemaphoreType.DMA
    hbm = pl.BlockSpec(memory_space=pl.ANY)
    out = jax.ShapeDtypeStruct(initial_gains.shape, f32)
    mixed = jax.ShapeDtypeStruct((2, groups, units, n_chan, n_st), f32)
    fits = jax.ShapeDtypeStruct((units, 8 * groups, n_st), f32)
    gains, coefs = pl.pallas_call(
        functools.partial(admm_kernel, (ns, m, n_ch, n_dir, n_base, groups, e)),
        out_shape=(mixed, fits),
        in_specs=[hbm, hbm, hbm, hbm, hbm],
        out_specs=(hbm, hbm),
        scratch_shapes=[
            pltpu.VMEM((ns, 2, CH, n_base), f32),
            pltpu.VMEM((groups, n_blk, 2, CH, BLOCK), f32),
            pltpu.VMEM((ns, 2, n_dir, CH, n_base), f32),
            pltpu.VMEM((ns, 2, n_base), jnp.int32),
            pltpu.VMEM((n_blk, n_st, 2 * BLOCK), bf16),
            pltpu.VMEM((n_blk, 2 * BLOCK, n_st), bf16),
            pltpu.VMEM((4 * per * CH, n_st), bf16),
            pltpu.VMEM((units, n_blk, 2 * CH, 2 * BLOCK), f32),
            pltpu.VMEM((n_blk, 2, CH, BLOCK), f32),
            pltpu.VMEM((6 * per * CH, n_st), f32),
            pltpu.VMEM((k_all, per, 3 * CH, n_st), f32),
            pltpu.VMEM((k_all, m - 1, e, 3 * CH, n_st), f32),
            pltpu.VMEM((n_dir, 2, CH, n_st), f32),
            pltpu.VMEM((groups, units, 2, CH, n_st), f32),
            pltpu.VMEM((k_all, e, 2, CH, n_st), f32),
            pltpu.VMEM((k_all, e, 2, CH, n_st), f32),
            pltpu.VMEM((k_all, e, 2, CH, n_st), f32),
            pltpu.VMEM((groups, 4, CH, 128), f32),
            pltpu.VMEM((2, n_c, e, 8 * groups, n_st), f32),
            pltpu.VMEM((2, n_c, n_ch - 1, e, 8 * groups, n_st), f32),
            pltpu.VMEM((2, n_c, e, 8 * groups, n_st), f32),
            pltpu.VMEM((2, n_c, e, 8 * groups, n_st), f32),
            pltpu.VMEM((n_c, e, 8 * groups, n_st), f32),
            dma((5,)),
            dma((n_c,)),
            dma((2,)),
            dma((2,)),
            dma((n_c,)),
            dma((n_c,)),
            dma((k_all, m - 1)),
            dma((k_all, m - 1)),
            dma((k_all, m - 1)),
            dma((k_all, m - 1)),
            dma((2, n_c, n_ch - 1)),
            dma((2, n_c, n_ch - 1)),
            dma((2, n_c)),
            dma((2, n_c)),
            dma((n_c, m - 1)),
            dma((n_c, m - 1)),
            dma((groups, n_c, 2)),
            dma((groups, n_c, 2)),
            dma((groups, n_c, 2)),
            dma((n_c,)),
        ],
        compiler_params=pltpu.CompilerParams(
            collective_id=0, has_side_effects=True, vmem_limit_bytes=62 * 2**20
        ),
        name="admm",
    )(vis, model, stations, initial_gains, unit_basis)
    coefs = coefs.reshape(n_dir, 8, n_st)
    block = n_dir // FINISH_STEPS
    whole = pl.BlockSpec((2, block, n_chan, n_st), lambda i: (0, i, 0, 0))
    return pl.pallas_call(
        functools.partial(finish_kernel, ns, groups),
        grid=(FINISH_STEPS,),
        out_shape=(out, out),
        in_specs=[
            pl.BlockSpec((2, groups, block // groups, n_chan, n_st), lambda i: (0, 0, i, 0, 0)),
            pl.BlockSpec((block, 8, n_st), lambda i: (i, 0, 0)),
            pl.BlockSpec(basis.shape, lambda i: (0, 0, 0, 0)),
        ],
        out_specs=(whole, whole),
        compiler_params=pltpu.CompilerParams(vmem_limit_bytes=62 * 2**20),
        name="finish",
    )(gains, coefs, basis)


def solution(mesh):
    placed = (
        P(None, "ch", "bl"),
        P(None, None, "ch", "bl"),
        P(None, "bl"),
        P(None, None, "ch", None),
    )
    return jax.shard_map(
        functools.partial(per_device, mesh.shape["bl"], mesh.shape["ch"]),
        mesh=mesh,
        in_specs=placed,
        out_specs=(P(None, None, "ch", None), P(None, None, "ch", None)),
        check_vma=False,
    )
```
